256 devices in a mesh: branch: 2 (over core), gi: 16 (over y_hi, z), gj: 8 (over x, y_lo).
Axes of the slice: x: 4, y: 4 (y_hi: 2, y_lo: 2; y = y_hi * 2 + y_lo), z: 8, core: 2. Of those that a mesh axis runs over, the one named last changes fastest.
Arguments:
- homolog_embedding: float32 [128, 256, 256], P(('branch', 'gj'), 'gi'), may hold values from -6 to 6
- pair_input_tensor: float32 [256, 256, 128], P('gi', ('branch', 'gj')), may hold values from -6 to 6
- layernorm_scales: float32 [4, 256], replicated, may hold values from 0.5 to 1.5
- pair_norm_gains: float32 [3, 128], replicated, may hold values from 0.5 to 1.5
- pair_bias_matrix: float32 [128, 8], replicated
- horizontal_qkvg_kernel: float32 [256, 1024], replicated, may hold values from -0.375 to 0.375
- horizontal_final_kernel: float32 [256, 256], replicated, may hold values from -0.375 to 0.375
- vertical_qkvg_kernel: float32 [256, 1024], replicated, may hold values from -0.375 to 0.375
- vertical_final_kernel: float32 [256, 256], replicated, may hold values from -0.375 to 0.375
- feedforward_expand_kernel: float32 [256, 1024], replicated, may hold values from -0.375 to 0.375
- feedforward_shrink_kernel: float32 [1024, 256], replicated, may hold values from -0.1875 to 0.1875
- dyadic_sides_kernel: float32 [256, 64], replicated, may hold values from -0.375 to 0.375
- outer_output_matrix: float32 [1024, 128], replicated, may hold values from -1 to 1
- triangle_input_matrix: float32 [128, 640], replicated, may hold values from -0.5 to 0.5
- triangle_output_matrix: float32 [128, 128], replicated, may hold values from -0.5 to 0.5
Outputs:
- alignment_output: float32 [128, 256, 256], P(('branch', 'gj'), 'gi')
- pair_output_tensor: float32 [256, 256, 128], P('gi', ('branch', 'gj'))
The draws below stay inside these ranges and needn't reach their ends.
All inputs are finite; a program needn't handle non-finite values.
Results may differ from the reference program's by a relative error of at most 0.0003.
Values sent between devices are 32-bit elements; how exact they have to be, the bound alone decides.
A program may use at most 64 MiB of HBM per device.

```python
import math
import jax
import jax.numpy as jnp
from jax import lax

EMBED_DIM = 256
CZ = 128
H = 8
HS = 32
PRODUCT_DIM = 32
HEADS_BY_SIZE = 256
HIDDEN_UNITS = 1024
HOMOLOG_NUMBER = 128
CHAIN_LENGTH = 256


def draw_pair_bias_matrix(key, part):
    base = jax.random.normal(key, (CZ, H), jnp.float32)
    return base * (2.0 / math.sqrt(CZ))


def levels(own_key, shape, shards, smallest, top_value):
    gain, own = 1.0, jax.random.fold_in(own_key, 6)
    for dim, shards_of in shards:
        steps = jnp.exp(jax.random.uniform(jax.random.fold_in(own, dim), (shards_of,), jnp.float32, smallest / len(shards), top_value / len(shards)))
        gain = gain * jnp.repeat(steps, shape[dim] // shards_of).reshape([-1 if axis == dim else 1 for axis in range(len(shape))])
    return gain


def scatter_about(own_key, dims, spread, most, pieces=(), kind=jnp.bfloat16):
    result = spread * jax.random.normal(own_key, dims, jnp.float32)
    if pieces:
        result = result * levels(own_key, dims, pieces, -0.22, 0.18)
    return jnp.clip(result, -most, most).astype(kind)


def setup_inputs(seed: int = 0) -> dict:
    key_list = jax.random.split(jax.random.key(seed), 16)
    homolog_embedding = scatter_about(key_list[0], (HOMOLOG_NUMBER, CHAIN_LENGTH, EMBED_DIM), 1.0, 6.0, ((0, 16), (1, 16)), jnp.float32)
    pair_input_tensor = scatter_about(key_list[1], (CHAIN_LENGTH, CHAIN_LENGTH, CZ), 1.0, 6.0, ((0, 16), (1, 16)), jnp.float32)
    layernorm_scales = jnp.clip(1.0 + 0.1 * jax.random.normal(key_list[2], (4, EMBED_DIM), jnp.float32), 0.5, 1.5)
    pair_norm_gains = jnp.clip(1.0 + 0.1 * jax.random.normal(key_list[3], (3, CZ), jnp.float32), 0.5, 1.5)
    pair_bias_matrix = draw_pair_bias_matrix(jax.random.fold_in(key_list[15], 71), 0)
    horizontal_qkvg_kernel = scatter_about(key_list[5], (EMBED_DIM, 4 * HEADS_BY_SIZE), EMBED_DIM ** -0.5, 0.375, (), jnp.float32)
    horizontal_final_kernel = scatter_about(key_list[6], (HEADS_BY_SIZE, EMBED_DIM), HEADS_BY_SIZE ** -0.5, 0.375, (), jnp.float32)
    vertical_qkvg_kernel = scatter_about(key_list[7], (EMBED_DIM, 4 * HEADS_BY_SIZE), EMBED_DIM ** -0.5, 0.375, (), jnp.float32)
    vertical_final_kernel = scatter_about(key_list[8], (HEADS_BY_SIZE, EMBED_DIM), HEADS_BY_SIZE ** -0.5, 0.375, (), jnp.float32)
    feedforward_expand_kernel = scatter_about(key_list[9], (EMBED_DIM, HIDDEN_UNITS), EMBED_DIM ** -0.5, 0.375, (), jnp.float32)
    feedforward_shrink_kernel = scatter_about(key_list[10], (HIDDEN_UNITS, EMBED_DIM), HIDDEN_UNITS ** -0.5, 0.1875, (), jnp.float32)
    dyadic_sides_kernel = scatter_about(key_list[11], (EMBED_DIM, 2 * PRODUCT_DIM), EMBED_DIM ** -0.5, 0.375, (), jnp.float32)
    outer_output_matrix = scatter_about(key_list[12], (PRODUCT_DIM * PRODUCT_DIM, CZ), PRODUCT_DIM ** -0.5, 1.0, (), jnp.float32)
    triangle_input_matrix = scatter_about(key_list[13], (CZ, 5 * CZ), CZ ** -0.5, 0.5, (), jnp.float32)
    triangle_output_matrix = scatter_about(key_list[14], (CZ, CZ), CZ ** -0.5, 0.5, (), jnp.float32)
    return {"homolog_embedding": homolog_embedding, "pair_input_tensor": pair_input_tensor, "layernorm_scales": layernorm_scales, "pair_norm_gains": pair_norm_gains, "pair_bias_matrix": pair_bias_matrix, "horizontal_qkvg_kernel": horizontal_qkvg_kernel, "horizontal_final_kernel": horizontal_final_kernel, "vertical_qkvg_kernel": vertical_qkvg_kernel, "vertical_final_kernel": vertical_final_kernel, "feedforward_expand_kernel": feedforward_expand_kernel, "feedforward_shrink_kernel": feedforward_shrink_kernel, "dyadic_sides_kernel": dyadic_sides_kernel, "outer_output_matrix": outer_output_matrix, "triangle_input_matrix": triangle_input_matrix, "triangle_output_matrix": triangle_output_matrix}


epsilon = 1e-05
highest = lax.Precision.HIGHEST

def layer_normalise(values, norm_gain):
    average = lax.optimization_barrier(jnp.mean(values, axis=-1, keepdims=True))
    centred = values - average
    variance = lax.optimization_barrier(jnp.mean(centred * centred, axis=-1, keepdims=True))
    return centred * lax.rsqrt(variance + epsilon) * norm_gain

def apply_projection(values, weight):
    return jnp.einsum('...c,cd->...d', values, weight, precision=highest)

def transition_update(values, norm_gain, feedforward_expand_kernel, feedforward_shrink_kernel):
    expanded = jax.nn.relu(apply_projection(layer_normalise(values, norm_gain), feedforward_expand_kernel))
    return values + apply_projection(expanded, feedforward_shrink_kernel)

def reference(homolog_embedding, pair_input_tensor, layernorm_scales, pair_norm_gains, pair_bias_matrix, horizontal_qkvg_kernel, horizontal_final_kernel, vertical_qkvg_kernel, vertical_final_kernel, feedforward_expand_kernel, feedforward_shrink_kernel, dyadic_sides_kernel, outer_output_matrix, triangle_input_matrix, triangle_output_matrix):
    bias_heads = jnp.transpose(apply_projection(layer_normalise(pair_input_tensor, pair_norm_gains[0]), pair_bias_matrix), (2, 0, 1))
    projected_values = apply_projection(layer_normalise(homolog_embedding, layernorm_scales[0]), horizontal_qkvg_kernel)
    queries = projected_values[..., :HEADS_BY_SIZE].reshape(HOMOLOG_NUMBER, CHAIN_LENGTH, H, HS)
    key_rows = projected_values[..., HEADS_BY_SIZE:2 * HEADS_BY_SIZE].reshape(HOMOLOG_NUMBER, CHAIN_LENGTH, H, HS)
    value_rows = projected_values[..., 2 * HEADS_BY_SIZE:3 * HEADS_BY_SIZE].reshape(HOMOLOG_NUMBER, CHAIN_LENGTH, H, HS)
    gate_row_values = projected_values[..., 3 * HEADS_BY_SIZE:]

    def row_single(inputs):
        query_row, key_row, value_row = inputs
        scores = jnp.einsum('ihd,jhd->hij', query_row, key_row, precision=highest) / math.sqrt(HS) + bias_heads
        weights = jax.nn.softmax(scores, axis=-1)
        return jnp.einsum('hij,jhd->ihd', weights, value_row, precision=highest)
    attention_result = lax.map(row_single, (queries, key_rows, value_rows)).reshape(HOMOLOG_NUMBER, CHAIN_LENGTH, HEADS_BY_SIZE)
    alignment_after_rows = homolog_embedding + apply_projection(jax.nn.sigmoid(gate_row_values) * attention_result, horizontal_final_kernel)
    projected_values = apply_projection(layer_normalise(alignment_after_rows, layernorm_scales[1]), vertical_qkvg_kernel)
    queries = jnp.transpose(projected_values[..., :HEADS_BY_SIZE].reshape(HOMOLOG_NUMBER, CHAIN_LENGTH, H, HS), (1, 0, 2, 3))
    key_rows = jnp.transpose(projected_values[..., HEADS_BY_SIZE:2 * HEADS_BY_SIZE].reshape(HOMOLOG_NUMBER, CHAIN_LENGTH, H, HS), (1, 0, 2, 3))
    value_rows = jnp.transpose(projected_values[..., 2 * HEADS_BY_SIZE:3 * HEADS_BY_SIZE].reshape(HOMOLOG_NUMBER, CHAIN_LENGTH, H, HS), (1, 0, 2, 3))
    gate_row_values = projected_values[..., 3 * HEADS_BY_SIZE:]

    def column_single(inputs):
        query_col, key_col, value_col = inputs
        scores = jnp.einsum('shd,thd->hst', query_col, key_col, precision=highest) / math.sqrt(HS)
        weights = jax.nn.softmax(scores, axis=-1)
        return jnp.einsum('hst,thd->shd', weights, value_col, precision=highest)
    attention_result = jnp.transpose(lax.map(column_single, (queries, key_rows, value_rows)), (1, 0, 2, 3)).reshape(HOMOLOG_NUMBER, CHAIN_LENGTH, HEADS_BY_SIZE)
    alignment_after_columns = alignment_after_rows + apply_projection(jax.nn.sigmoid(gate_row_values) * attention_result, vertical_final_kernel)
    alignment_output = transition_update(alignment_after_columns, layernorm_scales[2], feedforward_expand_kernel, feedforward_shrink_kernel)
    factor_pair = apply_projection(layer_normalise(alignment_output, layernorm_scales[3]), dyadic_sides_kernel)
    left_side = jnp.transpose(factor_pair[..., :PRODUCT_DIM], (1, 0, 2))
    right_side = jnp.transpose(factor_pair[..., PRODUCT_DIM:], (1, 0, 2))

    def outer_single(left_row):
        outer = jnp.einsum('sc,jsd->jcd', left_row, right_side, precision=highest) / HOMOLOG_NUMBER
        return apply_projection(outer.reshape(CHAIN_LENGTH, PRODUCT_DIM * PRODUCT_DIM), outer_output_matrix)
    pair_first = pair_input_tensor + lax.map(outer_single, left_side)
    projected_values = apply_projection(layer_normalise(pair_first, pair_norm_gains[1]), triangle_input_matrix)
    left_tri = jax.nn.sigmoid(projected_values[..., CZ:2 * CZ]) * projected_values[..., :CZ]
    right_tri = jax.nn.sigmoid(projected_values[..., 3 * CZ:4 * CZ]) * projected_values[..., 2 * CZ:3 * CZ]
    out_gate = projected_values[..., 4 * CZ:]
    product = jnp.einsum('ikc,jkc->ijc', left_tri, right_tri, precision=highest)
    pair_output_tensor = pair_first + jax.nn.sigmoid(out_gate) * apply_projection(layer_normalise(product, pair_norm_gains[2]), triangle_output_matrix)
    return (alignment_output, pair_output_tensor)
```

```python
import functools
import math

import jax
import jax.numpy as jnp
from jax import lax
from jax.experimental import pallas as pl
from jax.experimental.pallas import tpu as pltpu
from jax.sharding import PartitionSpec as P

F32, BF16 = jnp.float32, jnp.bfloat16
NN = (((1,), (0,)), ((), ()))
NT = (((1,), (1,)), ((), ()))
MESH = pl.DeviceIdType.MESH
EPS = 1e-05
ROOT = 1.0 / math.sqrt(32.0)


def roll(x, shift, axis):
    return pltpu.roll(x, shift, axis)


def split(x):
    hi = x.astype(BF16)
    return hi, (x - hi.astype(F32)).astype(BF16)


def dot(a, b, dims):
    return lax.dot_general(a, b, dims, preferred_element_type=F32)


def mm(a, b, dims=NN):
    return dot(a[0], b[0], dims) + (dot(a[0], b[1], dims) + dot(a[1], b[0], dims))


def norm(x, gain):
    centred = x - jnp.mean(x, axis=-1, keepdims=True)
    variance = jnp.mean(centred * centred, axis=-1, keepdims=True)
    return centred * lax.rsqrt(variance + EPS) * gain


def iota(shape, dim):
    return lax.broadcasted_iota(jnp.int32, shape, dim)


def swap_blocks(x, bits, lane_shift):
    sub, lane = iota(x.shape, 1), iota(x.shape, 2)
    for b in range(bits):
        rows, lanes = 1 << b, 1 << (lane_shift + b)
        sbit, lbit = (sub >> b) & 1, (lane >> (lane_shift + b)) & 1
        down = roll(roll(x, lanes, 2), 8 - rows, 1)
        up = roll(roll(x, 128 - lanes, 2), rows, 1)
        x = jnp.where(sbit == lbit, x, jnp.where(sbit == 0, down, up))
    return x


def f_bias(pair, gain, wb):
    wide = (iota((8, 128), 1) // 16 == iota((8, 128), 0)).astype(BF16)
    w = tuple(dot(part, wide, NN).astype(BF16) for part in split(wb))
    y = mm(split(norm(pair, gain)), w)
    y = jnp.where(iota(y.shape, 0) % 16 == iota(y.shape, 1) % 16, y, 0.0)
    return jnp.sum(y.reshape(16, 16, 128), axis=1)


def head_scores(k, q, h):
    own = iota(k[0].shape, 1) // 32 == h
    zero = jnp.zeros_like(k[0])
    return mm((jnp.where(own, k[0], zero), jnp.where(own, k[1], zero)), q, NT) * ROOT


def attend(scores, vt, h):
    weights = jnp.exp(scores - jnp.max(scores, axis=0, keepdims=True))
    total = jnp.sum(weights, axis=0, keepdims=True)
    rows = slice(32 * h, 32 * h + 32)
    return mm((vt[0][rows], vt[1][rows]), split(weights)) / total


def f_opm(left, right, wo):
    outer = (mm(split(left), split(right), NT) * (1.0 / 128.0)).reshape(16, 4, 8, 512)
    total = None
    for g in range(4):
        parts = [
            swap_blocks(outer[:, g, :, 128 * n : 128 * n + 128], 2, 5).reshape(128, 128)
            for n in range(4)
        ]
        term = mm(split(jnp.concatenate(parts, axis=0)), wo(g))
        total = term if total is None else total + term
    total = total.reshape(4, 16, 8, 256)
    halves = []
    for n in range(2):
        a, b = total[2 * n], total[2 * n + 1]
        even = a[..., :128] + roll(a[..., 128:], 4, 1)
        odd = b[..., 128:] + roll(b[..., :128], 4, 1)
        halves.append(jnp.where(iota(even.shape, 1) < 4, even, odd))
    return halves


def kernel(
    hom, pair, scales, pgains, wb, h_wq, h_wf, h_wv, h_wvf, h_we, h_ws, h_wd, h_wo, h_wt, h_wto,
    out_al, out_pair,
    wq, wf, wv, wvf, we, ws, wd, wo, wt, wto,
    bq, bf, bv, bvf, be, bs, bwd, bo, bt, bto,
    s_bias1, r_bias1, s_bias2, r_bias2, r_raw, gate, scores,
    s_att, r_att, first, s_col, r_col, s_al, r_al, s_ab, r_a, r_b,
    pf, gout, s_ta, s_tb, r_ta, r_tb, s_ba, s_bb, r_ba, r_bb, s_c, r_c, s_d, r_d,
    wsem, ssem, rsem,
):
    core, gi, gj = lax.axis_index("branch"), lax.axis_index("gi"), lax.axis_index("gj")
    bj = core * 8 + gj
    half, z = gi // 8, gi % 8

    def load(n, src, dst):
        copy = pltpu.make_async_copy(src, dst, wsem.at[n])
        copy.start()
        return copy

    loads = {"q": []}
    for b in range(4):
        column = pl.multiple_of(256 * b + 128 * half, 128)
        loads["q"].append(load(b, h_wq.at[:, pl.ds(column, 128)], wq.at[:, pl.ds(128 * b, 128)]))
    for n, (name, src, dst) in enumerate(
        (
            ("f", h_wf, wf), ("v", h_wv, wv), ("vf", h_wvf, wvf), ("e", h_we, we), ("s", h_ws, ws),
            ("d", h_wd, wd), ("o", h_wo, wo), ("t", h_wt, wt), ("to", h_wto, wto),
        )
    ):
        loads[name] = [load(4 + n, src, dst)]

    def ready(name, src, dst):
        for copy in loads[name]:
            copy.wait()
        depth = src.shape[0]

        @pl.loop(0, depth // 32)
        def _(n):
            rows = pl.ds(pl.multiple_of(n * 32, 32), 32)
            hi, lo = split(src[rows, :])
            dst[0, rows, :] = hi
            dst[1, rows, :] = lo

    def weight(ref, rows=slice(None), columns=slice(None)):
        return ref[0, rows, columns], ref[1, rows, columns]

    def on_gi(g):
        return {"gi": g}

    def on_bj(b):
        return {"branch": b // 8, "gj": b % 8}

    def cross(g):
        return {"gi": g, "branch": gi // 8, "gj": gi % 8}

    def each(count, me, one):
        @pl.loop(1, count)
        def _(d):
            one(lax.rem(me + d, count))

    def send(n, src, dst, device):
        pltpu.make_async_remote_copy(
            src_ref=src, dst_ref=dst, send_sem=ssem.at[n], recv_sem=rsem.at[n],
            device_id=device, device_id_type=MESH,
        ).start()

    def keep(n, src, dst):
        pltpu.make_async_copy(src, dst, rsem.at[n]).start()

    def exchange(n, me, device, src, dst):
        keep(n, src(me), dst)
        each(16, me, lambda peer: send(n, src(peer), dst, device(peer)))

    def eight(ref, b):
        return ref.at[:, pl.ds(pl.multiple_of(b * 8, 8), 8), :]

    def arrived(n, whole):
        pltpu.make_async_copy(whole, whole, rsem.at[n]).wait()

    def sent(n, most):
        pltpu.make_async_copy(most, most, ssem.at[n]).wait()

    barrier = pltpu.get_barrier_semaphore()

    def greet(device):
        pl.semaphore_signal(barrier, inc=1, device_id=device, device_id_type=MESH)

    each(16, gi, lambda g: greet(on_gi(g)))
    each(16, bj, lambda b: greet(on_bj(b)))
    each(16, bj, lambda b: greet({"gi": bj, "branch": b // 8, "gj": b % 8}))

    @pl.when(gi != bj)
    def _():
        greet({"gi": bj})

    pair2 = pair[...].reshape(256, 128)
    s_bias1[...] = f_bias(pair2, pgains[0:1, :], wb[...])

    pl.semaphore_wait(barrier, 45 + jnp.where(gi == bj, 0, 1))

    exchange(1, gi, on_gi, lambda g: s_bias1, r_bias1.at[gi])
    exchange(0, gi, on_gi, lambda g: hom.at[g % 8], r_raw.at[gi])
    ready("q", wq, bq)
    arrived(1, r_bias1)
    s_bias2[...] = r_bias1[...].reshape(256, 128).T.reshape(8, 16, 256)
    mine = s_bias2.at[pl.ds(half * 4, 4)]
    slot = r_bias2.at[:, pl.ds(pl.multiple_of(bj * 16, 16), 16), :]
    exchange(2, bj, on_bj, lambda b: mine, slot)

    arrived(0, r_raw)
    x = norm(r_raw[...].reshape(256, 256), scales[0:1, :])
    xs = split(x)
    q = split(mm(xs, weight(bq, columns=slice(0, 128))))
    k = split(mm(xs, weight(bq, columns=slice(128, 256))))
    vt = split(mm(xs, weight(bq, columns=slice(256, 384))).T)
    gate[...] = jax.nn.sigmoid(mm(xs, weight(bq, columns=slice(384, 512))))
    for h in range(4):
        scores[h] = head_scores(k, q, h)
    ready("f", wf, bf)
    arrived(2, r_bias2)
    heads = [attend(scores[h] + r_bias2[h], vt, h) for h in range(4)]
    att = gate[...] * jnp.concatenate(heads, axis=0).T
    s_att[...] = att.reshape(16, 16, 128)
    exchange(3, gi, on_gi, lambda g: s_att.at[g], r_att.at[gi])
    ready("v", wv, bv)
    ready("vf", wvf, bvf)

    arrived(3, r_att)
    a = r_att[...].reshape(256, 128)
    value = (
        hom[...].reshape(128, 256)
        + mm(split(a[:128]), weight(bf, slice(0, 128)))
        + mm(split(a[128:]), weight(bf, slice(128, 256)))
    )
    for n in range(2):
        lanes = slice(128 * n, 128 * n + 128)
        first[n] = value[:, lanes]
        for p in range(16):
            s_col[p, :, lanes] = first[n, pl.ds(p, 8, stride=16), :]
    exchange(4, bj, on_bj, lambda b: s_col.at[b], r_col.at[bj])
    ready("e", we, be)
    ready("s", ws, bs)

    arrived(4, r_col)
    col = r_col[...].reshape(128, 256)
    xs = split(norm(col, scales[1:2, :]))
    pieces = []
    for n in range(2):
        lanes = [slice(256 * b + 128 * n, 256 * b + 128 * n + 128) for b in range(4)]
        q = split(mm(xs, weight(bv, columns=lanes[0])))
        k = split(mm(xs, weight(bv, columns=lanes[1])))
        vt = split(mm(xs, weight(bv, columns=lanes[2])).T)
        g = jax.nn.sigmoid(mm(xs, weight(bv, columns=lanes[3])))
        heads = [attend(head_scores(k, q, h), vt, h) for h in range(4)]
        pieces.append(g * jnp.concatenate(heads, axis=0).T)
    second = (
        col
        + mm(split(pieces[0]), weight(bvf, slice(0, 128)))
        + mm(split(pieces[1]), weight(bvf, slice(128, 256)))
    )
    wide = jax.nn.relu(mm(split(norm(second, scales[2:3, :])), weight(be)))
    al = second + mm(split(wide), weight(bs))
    s_al[0], s_al[1] = al[:, :128], al[:, 128:]
    for copy in loads["d"]:
        copy.wait()
    factors = mm(split(norm(al, scales[3:4, :])), split(wd[...])).T
    s_ab[...] = factors.reshape(2, 32, 128)
    exchange(5, bj, on_bj, lambda b: s_ab.at[0], r_a.at[bj])

    @pl.loop(0, 16)
    def _(d):
        g = lax.rem(gi + d, 16)
        stays = jnp.logical_and(g == gi, gi == bj)

        @pl.when(stays)
        def _():
            keep(6, s_ab.at[1], r_b.at[bj])

        @pl.when(jnp.logical_not(stays))
        def _():
            send(6, s_ab.at[1], r_b.at[bj], cross(g))

    exchange(7, bj, on_bj, lambda b: eight(s_al, b), eight(r_al, bj))
    ready("o", wo, bo)
    ready("t", wt, bt)
    ready("to", wto, bto)

    arrived(5, r_a)
    arrived(6, r_b)

    def outer_weight(g):
        parts = [weight(bo, slice(256 * g + 128 * n, 256 * g + 128 * n + 128)) for n in range(2)]
        return tuple(jnp.concatenate([parts[0][m], parts[1][m]], axis=1) for m in range(2))

    updates = f_opm(r_a[...].reshape(512, 128), r_b[...].reshape(512, 128), outer_weight)
    for n in range(2):
        rows = slice(8 * n, 8 * n + 8)
        pf[:, rows, :] = pair[:, rows, :] + updates[n]
    xs = split(norm(pf[...].reshape(256, 128), pgains[1:2, :]))
    r = [mm(xs, weight(bt, columns=slice(128 * n, 128 * n + 128))) for n in range(5)]
    ta, tb = jax.nn.sigmoid(r[1]) * r[0], jax.nn.sigmoid(r[3]) * r[2]
    for n in range(2):
        s_ta[n] = ta[128 * n : 128 * n + 128].T
        s_tb[n] = tb[128 * n : 128 * n + 128].T
    gout[...] = jax.nn.sigmoid(r[4])

    exchange(8, bj, on_bj, lambda b: eight(s_ta, b), eight(r_ta, bj))
    exchange(9, bj, on_bj, lambda b: eight(s_tb, b), eight(r_tb, bj))

    def regroup(src, dst):
        for ih in range(2):
            for bh in range(2):
                block = jnp.stack([src[ih, pl.ds(64 * bh + c, 8, stride=8), :] for c in range(8)])
                dst[:, 8 * ih : 8 * ih + 8, 128 * bh : 128 * bh + 128] = swap_blocks(block, 3, 4)

    arrived(8, r_ta)
    regroup(r_ta, s_ba)
    exchange(10, gi, on_gi, lambda g: s_ba.at[g % 8], r_ba.at[gi])
    arrived(9, r_tb)
    regroup(r_tb, s_bb)
    keep(11, s_bb.at[z], r_bb.at[z])
    each(8, z, lambda other: send(11, s_bb.at[other], r_bb.at[z], on_gi(half * 8 + other)))
    arrived(10, r_ba)
    arrived(11, r_bb)
    x = mm(split(r_ba[...].reshape(256, 256)), split(r_bb[...].reshape(128, 256)), NT)
    s_c[...] = x.reshape(16, 16, 128)
    exchange(12, gi, on_gi, lambda g: s_c.at[g], r_c.at[gi])

    arrived(7, r_al)
    for row in range(8):
        for n in range(2):
            out_al[row, :, 128 * n : 128 * n + 128] = r_al[n, pl.ds(row, 16, stride=8), :]

    arrived(12, r_c)
    for hh in range(2):
        for ih in range(2):
            block = swap_blocks(r_c[8 * hh : 8 * hh + 8, 8 * ih : 8 * ih + 8, :], 3, 4)
            for c in range(8):
                s_d[ih, pl.ds(64 * hh + c, 8, stride=8), :] = block[c]
    exchange(13, bj, on_bj, lambda b: eight(s_d, b), eight(r_d, bj))
    arrived(13, r_d)
    x = norm(jnp.concatenate([r_d[0].T, r_d[1].T], axis=0), pgains[2:3, :])
    y = pf[...].reshape(256, 128) + gout[...] * mm(split(x), weight(bto))
    out_pair[...] = y.reshape(16, 16, 128)

    fifteen = pl.ds(0, 15)
    for n, ref in ((0, r_raw), (1, r_bias1), (3, s_att), (4, s_col), (5, r_a), (12, s_c)):
        sent(n, ref.at[fifteen])
    sent(2, r_bias2.at[:, pl.ds(0, 240), :])
    for n, ref in ((7, s_al), (8, s_ta), (9, s_tb), (13, s_d)):
        sent(n, ref.at[:, pl.ds(0, 120), :])
    sent(10, r_ba.at[fifteen])
    sent(11, r_bb.at[pl.ds(0, 7)])
    sent(6, r_b.at[fifteen])

    @pl.when(gi != bj)
    def _():
        sent(6, r_b.at[pl.ds(0, 1)])


def solution(mesh):
    def vmem(*shape, dtype=F32):
        return pltpu.VMEM(shape, dtype)

    widths = (
        (256, 512), (256, 256), (256, 1024), (256, 256), (256, 1024), (1024, 256), (256, 64),
        (1024, 128), (128, 640), (128, 128),
    )
    scratch = [vmem(*w) for w in widths] + [vmem(2, *w, dtype=BF16) for w in widths] + [
        vmem(16, 128), vmem(16, 16, 128), vmem(8, 16, 256), vmem(4, 256, 256), vmem(16, 16, 256),
        vmem(256, 128), vmem(4, 256, 256),
        vmem(16, 16, 128), vmem(16, 16, 128), vmem(2, 128, 128), vmem(16, 8, 256), vmem(16, 8, 256),
        vmem(2, 128, 128), vmem(2, 128, 128), vmem(2, 32, 128), vmem(16, 32, 128), vmem(16, 32, 128),
        vmem(16, 16, 128), vmem(256, 128), vmem(2, 128, 128), vmem(2, 128, 128), vmem(2, 128, 128), vmem(2, 128, 128),
        vmem(8, 16, 256), vmem(8, 16, 256), vmem(16, 16, 256), vmem(8, 16, 256),
        vmem(16, 16, 128), vmem(16, 16, 128), vmem(2, 128, 128), vmem(2, 128, 128),
        pltpu.SemaphoreType.DMA((13,)), pltpu.SemaphoreType.DMA((14,)), pltpu.SemaphoreType.DMA((14,)),
    ]

    def per_device(*args):
        return pl.pallas_call(
            kernel,
            out_shape=(
                jax.ShapeDtypeStruct((8, 16, 256), F32),
                jax.ShapeDtypeStruct((16, 16, 128), F32),
            ),
            in_specs=[pl.BlockSpec(memory_space=pltpu.VMEM)] * 5 + [pl.BlockSpec(memory_space=pl.ANY)] * 10,
            out_specs=(pl.BlockSpec(memory_space=pltpu.VMEM),) * 2,
            scratch_shapes=scratch,
            compiler_params=pltpu.CompilerParams(
                collective_id=0, has_side_effects=True, vmem_limit_bytes=56 * 1024 * 1024
            ),
            name="block",
        )(*args)

    msa, pairs = P(("branch", "gj"), "gi", None), P("gi", ("branch", "gj"), None)
    return jax.shard_map(
        per_device, mesh=mesh, in_specs=(msa, pairs) + (P(),) * 13, out_specs=(msa, pairs), check_vma=False
    )
```

```python
import functools
import math

import jax
import jax.numpy as jnp
from jax import lax
from jax.experimental import pallas as pl
from jax.experimental.pallas import tpu as pltpu
from jax.sharding import PartitionSpec as P

F32, BF16 = jnp.float32, jnp.bfloat16
NN = (((1,), (0,)), ((), ()))
NT = (((1,), (1,)), ((), ()))
MESH = pl.DeviceIdType.MESH
EPS = 1e-05
ROOT = 1.0 / math.sqrt(32.0)


def roll(x, shift, axis):
    return pltpu.roll(x, shift, axis)


def split(x):
    hi = x.astype(BF16)
    return hi, (x - hi.astype(F32)).astype(BF16)


def dot(a, b, dims):
    return lax.dot_general(a, b, dims, preferred_element_type=F32)


def mm(a, b, dims=NN):
    rows = a[0].shape[0]
    both = dot(jnp.concatenate(a, axis=0), b[0], dims)
    return both[:rows] + (dot(a[0], b[1], dims) + both[rows:])


def norm(x, gain):
    centred = x - jnp.mean(x, axis=-1, keepdims=True)
    variance = jnp.mean(centred * centred, axis=-1, keepdims=True)
    return centred * lax.rsqrt(variance + EPS) * gain


def iota(shape, dim):
    return lax.broadcasted_iota(jnp.int32, shape, dim)


def swap_blocks(x, bits, lane_shift):
    sub, lane = iota(x.shape, 1), iota(x.shape, 2)
    for b in range(bits):
        rows, lanes = 1 << b, 1 << (lane_shift + b)
        sbit, lbit = (sub >> b) & 1, (lane >> (lane_shift + b)) & 1
        down = roll(roll(x, lanes, 2), 8 - rows, 1)
        up = roll(roll(x, 128 - lanes, 2), rows, 1)
        x = jnp.where(sbit == lbit, x, jnp.where(sbit == 0, down, up))
    return x


def f_bias(pair, gain, wbt):
    lane, row = iota((256, 8), 0), iota((256, 8), 1)
    wide = (4 * (lane // 128) + lane // 16 % 4 == row).astype(BF16)
    w = tuple(dot(wide, part, NN).astype(BF16) for part in split(wbt))
    y = mm(split(norm(pair, gain)), w, NT)
    row, lane = iota(y.shape, 0), iota(y.shape, 1)
    own = jnp.logical_and(row % 16 == lane % 16, row // 128 == lane // 64 % 2)
    y = jnp.sum(jnp.where(own, y, 0.0).reshape(2, 8, 16, 256), axis=2)
    return y[0] + y[1]


def head_scores(k, q, h):
    own = iota(k[0].shape, 1) // 32 == h
    zero = jnp.zeros_like(k[0])
    return mm((jnp.where(own, k[0], zero), jnp.where(own, k[1], zero)), q, NT) * ROOT


def attend(scores, vt, h):
    weights = jnp.exp(scores - jnp.max(scores, axis=0, keepdims=True))
    total = jnp.sum(weights, axis=0, keepdims=True)
    rows = slice(32 * h, 32 * h + 32)
    return mm((vt[0][rows], vt[1][rows]), split(weights)) / total


def f_opm(left, right, wo):
    outer = (mm(split(left), split(right), NT) * (1.0 / 128.0)).reshape(16, 4, 8, 512)
    total = None
    for g in range(4):
        parts = [
            swap_blocks(outer[:, g, :, 128 * n : 128 * n + 128], 2, 5).reshape(128, 128)
            for n in range(4)
        ]
        term = mm(split(jnp.concatenate(parts, axis=0)), wo(g))
        total = term if total is None else total + term
    total = total.reshape(4, 16, 8, 256)
    halves = []
    for n in range(2):
        a, b = total[2 * n], total[2 * n + 1]
        even = a[..., :128] + roll(a[..., 128:], 4, 1)
        odd = b[..., 128:] + roll(b[..., :128], 4, 1)
        halves.append(jnp.where(iota(even.shape, 1) < 4, even, odd))
    return halves


def kernel(
    h_hom, h_pair, h_scales, h_pgains, h_wb, h_wq, h_wf, h_wv, h_wvf, h_we, h_ws, h_wd, h_wo, h_wt, h_wto,
    out_al, out_pair,
    hom, pair, scales, pgains, wb,
    wq, wf, wv, wvf, we, ws, wd, wo, wt, wto,
    bq, bf, bv, bvf, be, bs, bo, bt, bto,
    s_bias1, r_bias1, s_bias2, r_bias2, r_raw, gate, scores,
    s_att, r_att, first, s_col, r_col, s_al, r_al, s_ab, r_a, r_b,
    pf, gout, s_ta, s_tb, r_ta, r_tb, s_ba, s_bb, r_ba, r_bb, s_c, r_c, s_d, r_d,
    wsem, ssem, rsem, bsem,
):
    core, gi, gj = lax.axis_index("branch"), lax.axis_index("gi"), lax.axis_index("gj")
    bj = core * 8 + gj
    half, z = gi // 8, gi % 8

    def on_gi(g):
        return {"gi": g}

    def on_bj(b):
        return {"branch": b // 8, "gj": b % 8}

    def cross(g):
        return {"gi": g, "branch": gi // 8, "gj": gi % 8}

    def each(count, me, one):
        @pl.loop(1, count)
        def _(d):
            one(lax.rem(me + d, count))

    barrier = pltpu.get_barrier_semaphore()

    def greet(device):
        pl.semaphore_signal(barrier, inc=1, device_id=device, device_id_type=MESH)

    each(16, gi, lambda g: greet(on_gi(g)))
    each(16, bj, lambda b: greet(on_bj(b)))

    def load(n, src, dst):
        copy = pltpu.make_async_copy(src, dst, wsem.at[n])
        copy.start()
        return copy

    loads = {}
    for n, (name, src, dst) in enumerate(
        (
            ("pair", h_pair, pair), ("pgains", h_pgains, pgains), ("b", h_wb, wb),
            ("hom", h_hom, hom), ("scales", h_scales, scales),
        )
    ):
        loads[name] = load(14 + n, src, dst)

    loads["q"] = []
    for b in range(4):
        column = pl.multiple_of(256 * b + 128 * half, 128)
        loads["q"].append(load(b, h_wq.at[:, pl.ds(column, 128)], wq.at[:, pl.ds(128 * b, 128)]))
    for n, (name, src, dst) in enumerate(
        (
            ("f", h_wf, wf), ("v", h_wv, wv), ("vf", h_wvf, wvf), ("e", h_we, we), ("s", h_ws, ws),
            ("d", h_wd, wd), ("o", h_wo, wo), ("t", h_wt, wt), ("to", h_wto, wto),
        )
    ):
        loads[name] = [load(4 + n, src, dst)]

    def ready(name, src, dst):
        for copy in loads[name]:
            copy.wait()
        depth = src.shape[0]

        @pl.loop(0, depth // 32)
        def _(n):
            rows = pl.ds(pl.multiple_of(n * 32, 32), 32)
            hi, lo = split(src[rows, :])
            dst[0, rows, :] = hi
            dst[1, rows, :] = lo

    def weight(ref, rows=slice(None), columns=slice(None)):
        return ref[0, rows, columns], ref[1, rows, columns]

    def send(n, src, dst, device):
        pltpu.make_async_remote_copy(
            src_ref=src, dst_ref=dst, send_sem=ssem.at[n], recv_sem=rsem.at[n],
            device_id=device, device_id_type=MESH,
        ).start()

    def keep(n, src, dst):
        pltpu.make_async_copy(src, dst, rsem.at[n]).start()

    def exchange(n, me, device, src, dst):
        keep(n, src(me), dst)
        each(16, me, lambda peer: send(n, src(peer), dst, device(peer)))

    def eight(ref, b):
        return ref.at[:, pl.ds(pl.multiple_of(b * 8, 8), 8), :]

    def arrived(n, whole):
        pltpu.make_async_copy(whole, whole, rsem.at[n]).wait()

    def sent(n, most):
        pltpu.make_async_copy(most, most, ssem.at[n]).wait()

    for name in ("pair", "pgains", "b"):
        loads[name].wait()
    bias = f_bias(pair[...].reshape(256, 128), pgains[0:1, :], wb[...])
    s_bias1[0], s_bias1[1] = bias[:, :128], bias[:, 128:]
    pl.semaphore_wait(barrier, 30)
    exchange(1, gi, on_gi, lambda g: s_bias1.at[g // 8], r_bias1.at[gi])
    loads["hom"].wait()
    exchange(0, gi, on_gi, lambda g: hom.at[g % 8], r_raw.at[:, gi])
    ready("q", wq, bq)
    arrived(1, r_bias1)
    turned = r_bias1[...].reshape(128, 128).T
    for ih in range(2):
        s_bias2[:, :, :, 128 * ih : 128 * ih + 128] = turned[64 * ih : 64 * ih + 64].reshape(4, 2, 8, 128)

    def slot(branch, j):
        return r_bias2.at[:, :, pl.ds(pl.multiple_of(branch * 64 + j * 8, 8), 8), :]

    def pass_on(n, src, j, device):
        pltpu.make_async_remote_copy(
            src_ref=src, dst_ref=slot(core, j), send_sem=ssem.at[2], recv_sem=bsem.at[n],
            device_id=device, device_id_type=MESH,
        ).start()

    sibling = {"branch": 1 - core}

    @pl.loop(1, 8)
    def _(d):
        pass_on(d, s_bias2, gj, {"gj": lax.rem(gj + d, 8)})

    pass_on(0, s_bias2, gj, sibling)
    keep(2, s_bias2, slot(core, gj))

    @pl.loop(1, 8)
    def _(d):
        j = lax.rem(gj + 8 - d, 8)
        pltpu.make_async_copy(slot(core, j), slot(core, j), bsem.at[d]).wait()
        pass_on(7 + d, slot(core, j), j, sibling)

    arrived(0, r_raw)
    loads["scales"].wait()
    x = norm(r_raw[...].reshape(256, 256), scales[0:1, :])
    xs = split(x)
    q = split(mm(xs, weight(bq, columns=slice(0, 128))))
    k = split(mm(xs, weight(bq, columns=slice(128, 256))))
    vt = split(mm(xs, weight(bq, columns=slice(256, 384))).T)
    gate[...] = jax.nn.sigmoid(mm(xs, weight(bq, columns=slice(384, 512))))
    for h in range(4):
        scores[h] = head_scores(k, q, h)
    ready("f", wf, bf)
    arrived(2, s_bias2)
    for d in range(8):
        j = lax.rem(gj + 8 - d, 8)
        pltpu.make_async_copy(slot(1 - core, j), slot(1 - core, j), bsem.at[7 + d if d else 0]).wait()
    heads = [attend(scores[h] + r_bias2[h].reshape(256, 256), vt, h) for h in range(4)]
    att = gate[...] * jnp.concatenate(heads, axis=0).T
    s_att[...] = att.reshape(2, 16, 8, 128)
    exchange(3, gi, on_gi, lambda g: s_att.at[:, g], r_att.at[gi])
    ready("v", wv, bv)
    ready("vf", wvf, bvf)

    arrived(3, r_att)
    a = r_att[...].reshape(256, 128)
    value = (
        hom[...].reshape(128, 256)
        + mm(split(a[:128]), weight(bf, slice(0, 128)))
        + mm(split(a[128:]), weight(bf, slice(128, 256)))
    )
    for n in range(2):
        lanes = slice(128 * n, 128 * n + 128)
        first[n] = value[:, lanes]
        for p in range(16):
            s_col[p, :, lanes] = first[n, pl.ds(p, 8, stride=16), :]
    exchange(4, bj, on_bj, lambda b: s_col.at[b], r_col.at[bj])
    ready("e", we, be)
    ready("s", ws, bs)

    arrived(4, r_col)
    col = r_col[...].reshape(128, 256)
    xs = split(norm(col, scales[1:2, :]))
    pieces = []
    for n in range(2):
        lanes = [slice(256 * b + 128 * n, 256 * b + 128 * n + 128) for b in range(4)]
        q = split(mm(xs, weight(bv, columns=lanes[0])))
        k = split(mm(xs, weight(bv, columns=lanes[1])))
        vt = split(mm(xs, weight(bv, columns=lanes[2])).T)
        g = jax.nn.sigmoid(mm(xs, weight(bv, columns=lanes[3])))
        heads = [attend(head_scores(k, q, h), vt, h) for h in range(4)]
        pieces.append(g * jnp.concatenate(heads, axis=0).T)
    second = (
        col
        + mm(split(pieces[0]), weight(bvf, slice(0, 128)))
        + mm(split(pieces[1]), weight(bvf, slice(128, 256)))
    )
    wide = jax.nn.relu(mm(split(norm(second, scales[2:3, :])), weight(be)))
    al = second + mm(split(wide), weight(bs))
    s_al[0], s_al[1] = al[:, :128], al[:, 128:]
    for copy in loads["d"]:
        copy.wait()
    factors = mm(split(wd[...]), split(norm(al, scales[3:4, :])), NT)
    s_ab[...] = factors.reshape(2, 32, 128)
    exchange(5, bj, on_bj, lambda b: s_ab.at[0], r_a.at[bj])

    @pl.loop(0, 16)
    def _(d):
        g = lax.rem(gi + d, 16)
        stays = jnp.logical_and(g == gi, gi == bj)

        @pl.when(stays)
        def _():
            keep(6, s_ab.at[1], r_b.at[bj])

        @pl.when(jnp.logical_not(stays))
        def _():
            send(6, s_ab.at[1], r_b.at[bj], cross(g))

    exchange(7, bj, on_bj, lambda b: eight(s_al, b), eight(r_al, bj))
    ready("o", wo, bo)
    ready("t", wt, bt)
    ready("to", wto, bto)

    arrived(5, r_a)
    arrived(6, r_b)

    def outer_weight(g):
        parts = [weight(bo, slice(256 * g + 128 * n, 256 * g + 128 * n + 128)) for n in range(2)]
        return tuple(jnp.concatenate([parts[0][m], parts[1][m]], axis=1) for m in range(2))

    updates = f_opm(r_a[...].reshape(512, 128), r_b[...].reshape(512, 128), outer_weight)
    for n in range(2):
        rows = slice(8 * n, 8 * n + 8)
        pf[:, rows, :] = pair[:, rows, :] + updates[n]
    xs = split(norm(pf[...].reshape(256, 128), pgains[1:2, :]))
    r = [mm(xs, weight(bt, columns=slice(128 * n, 128 * n + 128))) for n in range(5)]
    ta, tb = jax.nn.sigmoid(r[1]) * r[0], jax.nn.sigmoid(r[3]) * r[2]
    for n in range(2):
        s_ta[n] = ta[128 * n : 128 * n + 128].T
        s_tb[n] = tb[128 * n : 128 * n + 128].T
    gout[...] = jax.nn.sigmoid(r[4])

    exchange(8, bj, on_bj, lambda b: eight(s_ta, b), eight(r_ta, bj))
    exchange(9, bj, on_bj, lambda b: eight(s_tb, b), eight(r_tb, bj))

    def regroup(src, dst):
        for ih in range(2):
            for bh in range(2):
                block = jnp.stack([src[ih, pl.ds(64 * bh + c, 8, stride=8), :] for c in range(8)])
                dst[:, 8 * ih : 8 * ih + 8, 128 * bh : 128 * bh + 128] = swap_blocks(block, 3, 4)

    arrived(8, r_ta)
    regroup(r_ta, s_ba)
    exchange(10, gi, on_gi, lambda g: s_ba.at[g % 8], r_ba.at[gi])
    arrived(9, r_tb)
    regroup(r_tb, s_bb)
    keep(11, s_bb.at[z], r_bb.at[z])
    each(8, z, lambda other: send(11, s_bb.at[other], r_bb.at[z], on_gi(half * 8 + other)))
    arrived(10, r_ba)
    arrived(11, r_bb)
    x = mm(split(r_ba[...].reshape(256, 256)), split(r_bb[...].reshape(128, 256)), NT)
    s_c[...] = x.reshape(16, 16, 128)
    exchange(12, gi, on_gi, lambda g: s_c.at[g], r_c.at[gi])

    arrived(7, r_al)
    for row in range(8):
        for n in range(2):
            out_al[row, :, 128 * n : 128 * n + 128] = r_al[n, pl.ds(row, 16, stride=8), :]

    arrived(12, r_c)
    for hh in range(2):
        for ih in range(2):
            block = swap_blocks(r_c[8 * hh : 8 * hh + 8, 8 * ih : 8 * ih + 8, :], 3, 4)
            for c in range(8):
                s_d[ih, pl.ds(64 * hh + c, 8, stride=8), :] = block[c]
    exchange(13, bj, on_bj, lambda b: eight(s_d, b), eight(r_d, bj))
    arrived(13, r_d)
    x = norm(jnp.concatenate([r_d[0].T, r_d[1].T], axis=0), pgains[2:3, :])
    y = pf[...].reshape(256, 128) + gout[...] * mm(split(x), weight(bto))
    out_pair[...] = y.reshape(16, 16, 128)

    fifteen = pl.ds(0, 15)
    for n, ref in ((1, r_bias1), (3, r_att), (4, s_col), (5, r_a), (12, s_c)):
        sent(n, ref.at[fifteen])
    sent(0, r_raw.at[:, fifteen])
    sent(2, r_bias2.at[:, :, pl.ds(0, 120), :])
    for n, ref in ((7, s_al), (8, s_ta), (9, s_tb), (13, s_d)):
        sent(n, ref.at[:, pl.ds(0, 120), :])
    sent(10, r_ba.at[fifteen])
    sent(11, r_bb.at[pl.ds(0, 7)])
    sent(6, r_b.at[fifteen])

    @pl.when(gi != bj)
    def _():
        sent(6, r_b.at[pl.ds(0, 1)])


def solution(mesh):
    def vmem(*shape, dtype=F32):
        return pltpu.VMEM(shape, dtype)

    widths = (
        (256, 512), (256, 256), (256, 1024), (256, 256), (256, 1024), (1024, 256), (64, 256),
        (1024, 128), (128, 640), (128, 128),
    )
    small = ((8, 2, 8, 256), (16, 16, 128), (4, 256), (3, 128), (8, 128))
    scratch = [vmem(*w) for w in small + widths]
    scratch += [vmem(2, *w, dtype=BF16) for w in widths if w != (64, 256)] + [
        vmem(2, 8, 128), vmem(16, 8, 128), vmem(4, 2, 8, 256), vmem(4, 2, 128, 256), vmem(2, 16, 8, 256),
        vmem(256, 128), vmem(4, 256, 256),
        vmem(2, 16, 8, 128), vmem(16, 2, 8, 128), vmem(2, 128, 128), vmem(16, 8, 256), vmem(16, 8, 256),
        vmem(2, 128, 128), vmem(2, 128, 128), vmem(2, 32, 128), vmem(16, 32, 128), vmem(16, 32, 128),
        vmem(16, 16, 128), vmem(256, 128), vmem(2, 128, 128), vmem(2, 128, 128), vmem(2, 128, 128), vmem(2, 128, 128),
        vmem(8, 16, 256), vmem(8, 16, 256), vmem(16, 16, 256), vmem(8, 16, 256),
        vmem(16, 16, 128), vmem(16, 16, 128), vmem(2, 128, 128), vmem(2, 128, 128),
        pltpu.SemaphoreType.DMA((19,)), pltpu.SemaphoreType.DMA((14,)), pltpu.SemaphoreType.DMA((14,)),
        pltpu.SemaphoreType.DMA((15,)),
    ]

    def per_device(*args):
        args = list(args)
        args[0] = args[0].reshape(8, 2, 8, 256)
        args[4], args[11] = args[4].T, args[11].T
        return pl.pallas_call(
            kernel,
            out_shape=(
                pltpu.VMEM((8, 16, 256), F32),
                pltpu.VMEM((16, 16, 128), F32),
            ),
            in_specs=[pl.BlockSpec(memory_space=pl.ANY)] * 15,
            out_specs=(pl.BlockSpec(memory_space=pltpu.VMEM),) * 2,
            scratch_shapes=scratch,
            compiler_params=pltpu.CompilerParams(
                collective_id=0, has_side_effects=True, vmem_limit_bytes=56 * 1024 * 1024
            ),
            name="block",
        )(*args)

    msa, pairs = P(("branch", "gj"), "gi", None), P("gi", ("branch", "gj"), None)
    return jax.shard_map(
        per_device, mesh=mesh, in_specs=(msa, pairs) + (P(),) * 13, out_specs=(msa, pairs), check_vma=False
    )
```

```python
import functools
import math

import jax
import jax.numpy as jnp
from jax import lax
from jax.experimental import pallas as pl
from jax.experimental.pallas import tpu as pltpu
from jax.sharding import PartitionSpec as P

F32, BF16 = jnp.float32, jnp.bfloat16
NN = (((1,), (0,)), ((), ()))
NT = (((1,), (1,)), ((), ()))
MESH = pl.DeviceIdType.MESH
EPS = 1e-05
ROOT = 1.0 / math.sqrt(32.0)


def roll(x, shift, axis):
    return pltpu.roll(x, shift, axis)


def split(x):
    hi = x.astype(BF16)
    return hi, (x - hi.astype(F32)).astype(BF16)


def dot(a, b, dims):
    return lax.dot_general(a, b, dims, preferred_element_type=F32)


def mm(a, b, dims=NN):
    rows = a[0].shape[0]
    both = dot(jnp.concatenate(a, axis=0), b[0], dims)
    return both[:rows] + (dot(a[0], b[1], dims) + both[rows:])


def norm(x, gain):
    centred = x - jnp.mean(x, axis=-1, keepdims=True)
    variance = jnp.mean(centred * centred, axis=-1, keepdims=True)
    return centred * lax.rsqrt(variance + EPS) * gain


def iota(shape, dim):
    return lax.broadcasted_iota(jnp.int32, shape, dim)


def swap_blocks(x, bits, lane_shift):
    sub, lane = iota(x.shape, 1), iota(x.shape, 2)
    for b in range(bits):
        rows, lanes = 1 << b, 1 << (lane_shift + b)
        sbit, lbit = (sub >> b) & 1, (lane >> (lane_shift + b)) & 1
        down = roll(roll(x, lanes, 2), 8 - rows, 1)
        up = roll(roll(x, 128 - lanes, 2), rows, 1)
        x = jnp.where(sbit == lbit, x, jnp.where(sbit == 0, down, up))
    return x


def f_bias(pair, gain, wbt):
    lane, row = iota((256, 8), 0), iota((256, 8), 1)
    wide = (4 * (lane // 128) + lane // 16 % 4 == row).astype(BF16)
    w = tuple(dot(wide, part, NN).astype(BF16) for part in split(wbt))
    y = mm(split(norm(pair, gain)), w, NT)
    row, lane = iota(y.shape, 0), iota(y.shape, 1)
    own = jnp.logical_and(row % 16 == lane % 16, row // 128 == lane // 64 % 2)
    y = jnp.sum(jnp.where(own, y, 0.0).reshape(2, 8, 16, 256), axis=2)
    return y[0] + y[1]


def head_scores(k, q, h):
    own = iota(k[0].shape, 1) // 32 == h
    zero = jnp.zeros_like(k[0])
    return mm((jnp.where(own, k[0], zero), jnp.where(own, k[1], zero)), q, NT) * ROOT


def attend(scores, vt, h):
    weights = jnp.exp(scores - jnp.max(scores, axis=0, keepdims=True))
    total = jnp.sum(weights, axis=0, keepdims=True)
    rows = slice(32 * h, 32 * h + 32)
    return mm((vt[0][rows], vt[1][rows]), split(weights)) / total


def f_opm(left, right, wo):
    outer = (mm(split(left), split(right), NT) * (1.0 / 128.0)).reshape(16, 4, 8, 512)
    total = None
    for g in range(4):
        parts = [
            swap_blocks(outer[:, g, :, 128 * n : 128 * n + 128], 2, 5).reshape(128, 128)
            for n in range(4)
        ]
        term = mm(split(jnp.concatenate(parts, axis=0)), wo(g))
        total = term if total is None else total + term
    total = total.reshape(4, 16, 8, 256)
    halves = []
    for n in range(2):
        a, b = total[2 * n], total[2 * n + 1]
        even = a[..., :128] + roll(a[..., 128:], 4, 1)
        odd = b[..., 128:] + roll(b[..., :128], 4, 1)
        halves.append(jnp.where(iota(even.shape, 1) < 4, even, odd))
    return halves


def kernel(
    h_hom, h_pair, h_scales, h_pgains, h_wb, h_wq, h_wf, h_wv, h_wvf, h_we, h_ws, h_wd, h_wo, h_wt, h_wto,
    out_al, out_pair,
    hom, pair, scales, pgains, wb,
    wq, wf, wv, wvf, we, ws, wd, wo, wt, wto,
    bq, bf, bv, bvf, be, bs, bo, bt, bto,
    s_bias1, r_bias1, s_bias2, r_bias2, r_raw, gate, scores,
    s_att, r_att, first, s_col, r_col, s_al, r_al, s_ab, r_a, r_b,
    pf, gout, s_ta, s_tb, r_ta, r_tb, s_ba, s_bb, r_ba, r_bb, s_d, r_d,
    wsem, ssem, rsem, bsem,
):
    core, gi, gj = lax.axis_index("branch"), lax.axis_index("gi"), lax.axis_index("gj")
    bj = core * 8 + gj
    half, z = gi // 8, gi % 8

    def on_gi(g):
        return {"gi": g}

    def on_bj(b):
        return {"branch": b // 8, "gj": b % 8}

    def cross(g):
        return {"gi": g, "branch": gi // 8, "gj": gi % 8}

    gx, gy = gj // 2, gj % 2

    def flip(bit, where):
        return where if bit == 0 else 1 - where

    def gi_peers():
        steps = sorted(((dy, dz) for dy in range(2) for dz in range(8)), key=lambda s: -2 * s[0] - min(s[1], 8 - s[1]))
        return [flip(dy, half) * 8 + (z + dz) % 8 for dy, dz in steps[:-1]]

    def gj_peers():
        steps = sorted(((dx, dy) for dx in range(4) for dy in range(2)), key=lambda s: -s[1] - min(s[0], 4 - s[0]))
        return [((gx + dx) % 4 if dx else gx, flip(dy, gy)) for dx, dy in steps]

    def bj_peers():
        own = gj_peers()
        every = [flip(dc, core) * 8 + px * 2 + py for px, py in own for dc in (1, 0)]
        return every[:-1]

    def each(peers, one):
        for peer in peers:
            one(peer)

    barrier = pltpu.get_barrier_semaphore()

    def greet(device):
        pl.semaphore_signal(barrier, inc=1, device_id=device, device_id_type=MESH)

    each(gi_peers(), lambda g: greet(on_gi(g)))
    each(bj_peers(), lambda b: greet(on_bj(b)))

    def load(n, src, dst):
        copy = pltpu.make_async_copy(src, dst, wsem.at[n])
        copy.start()
        return copy

    loads = {}
    for n, (name, src, dst) in enumerate(
        (
            ("pair", h_pair, pair), ("pgains", h_pgains, pgains), ("b", h_wb, wb),
            ("hom", h_hom, hom), ("scales", h_scales, scales),
        )
    ):
        loads[name] = load(14 + n, src, dst)

    loads["q"] = []
    for b in range(4):
        column = pl.multiple_of(256 * b + 128 * half, 128)
        loads["q"].append(load(b, h_wq.at[:, pl.ds(column, 128)], wq.at[:, pl.ds(128 * b, 128)]))
    for n, (name, src, dst) in enumerate(
        (
            ("f", h_wf, wf), ("v", h_wv, wv), ("vf", h_wvf, wvf), ("e", h_we, we), ("s", h_ws, ws),
            ("d", h_wd, wd), ("o", h_wo, wo), ("t", h_wt, wt), ("to", h_wto, wto),
        )
    ):
        loads[name] = [load(4 + n, src, dst)]

    def ready(name, src, dst):
        for copy in loads[name]:
            copy.wait()
        depth = src.shape[0]

        @pl.loop(0, depth // 32)
        def _(n):
            rows = pl.ds(pl.multiple_of(n * 32, 32), 32)
            hi, lo = split(src[rows, :])
            dst[0, rows, :] = hi
            dst[1, rows, :] = lo

    def weight(ref, rows=slice(None), columns=slice(None)):
        return ref[0, rows, columns], ref[1, rows, columns]

    def send(n, src, dst, device):
        pltpu.make_async_remote_copy(
            src_ref=src, dst_ref=dst, send_sem=ssem.at[n], recv_sem=rsem.at[n],
            device_id=device, device_id_type=MESH,
        ).start()

    def keep(n, src, dst):
        pltpu.make_async_copy(src, dst, rsem.at[n]).start()

    def exchange(n, me, device, src, dst):
        peers = gi_peers() if device is on_gi else bj_peers()
        each(peers, lambda peer: send(n, src(peer), dst, device(peer)))
        keep(n, src(me), dst)

    def far_first(one):
        @pl.loop(0, 7)
        def _(k):
            there = (z + jnp.where(k % 2 == 1, 4 - (k + 1) // 2, 4 + k // 2)) % 8
            one((1 - half) * 8 + there, False)
            one(half * 8 + there, False)

        one((1 - half) * 8 + z, False)
        one(gi, True)

    def eight(ref, b):
        return ref.at[:, pl.ds(pl.multiple_of(b * 8, 8), 8), :]

    def arrived(n, whole):
        pltpu.make_async_copy(whole, whole, rsem.at[n]).wait()

    def sent(n, most):
        pltpu.make_async_copy(most, most, ssem.at[n]).wait()

    for name in ("pair", "pgains", "b"):
        loads[name].wait()
    bias = f_bias(pair[...].reshape(256, 128), pgains[0:1, :], wb[...])
    s_bias1[0], s_bias1[1] = bias[:, :128], bias[:, 128:]
    pl.semaphore_wait(barrier, 30)
    exchange(1, gi, on_gi, lambda g: s_bias1.at[g // 8], r_bias1.at[gi])
    loads["hom"].wait()
    exchange(0, gi, on_gi, lambda g: hom.at[g % 8], r_raw.at[:, gi])
    ready("q", wq, bq)
    value = hom[...].reshape(128, 256)
    for n in range(2):
        lanes = slice(128 * n, 128 * n + 128)
        first[n] = value[:, lanes]
        for p in range(16):
            s_col[p, :, lanes] = first[n, pl.ds(p, 8, stride=16), :]
    arrived(1, r_bias1)
    turned = r_bias1[...].reshape(128, 128).T
    for ih in range(2):
        s_bias2[:, :, :, 128 * ih : 128 * ih + 128] = turned[64 * ih : 64 * ih + 64].reshape(4, 2, 8, 128)

    def slot(branch, j):
        return r_bias2.at[:, :, pl.ds(pl.multiple_of(branch * 64 + j * 8, 8), 8), :]

    def pass_on(n, src, j, device):
        pltpu.make_async_remote_copy(
            src_ref=src, dst_ref=slot(core, j), send_sem=ssem.at[2], recv_sem=bsem.at[n],
            device_id=device, device_id_type=MESH,
        ).start()

    sibling = {"branch": 1 - core}

    to = [(px * 2 + py) for px, py in gj_peers()]
    steps = sorted(((dx, dy) for dx in range(4) for dy in range(2)), key=lambda s: -s[1] - min(s[0], 4 - s[0]))
    senders = [((gx + 4 - dx) % 4 * 2 + flip(dy, gy)) for dx, dy in steps]
    for d in range(7):
        pass_on(d + 1, s_bias2, gj, {"gj": to[d]})
    pass_on(0, s_bias2, gj, sibling)
    keep(2, s_bias2, slot(core, gj))
    for d in range(7):
        j = senders[d]
        pltpu.make_async_copy(slot(core, j), slot(core, j), bsem.at[d + 1]).wait()
        pass_on(8 + d, slot(core, j), j, sibling)

    exchange(4, bj, on_bj, lambda b: s_col.at[b], r_col.at[bj])

    arrived(0, r_raw)
    loads["scales"].wait()
    x = norm(r_raw[...].reshape(256, 256), scales[0:1, :])
    xs = split(x)
    q = split(mm(xs, weight(bq, columns=slice(0, 128))))
    k = split(mm(xs, weight(bq, columns=slice(128, 256))))
    vt = split(mm(xs, weight(bq, columns=slice(256, 384))).T)
    gate[...] = jax.nn.sigmoid(mm(xs, weight(bq, columns=slice(384, 512))))
    for h in range(4):
        scores[h] = head_scores(k, q, h)
    ready("f", wf, bf)
    arrived(2, s_bias2)
    for n, j in enumerate([gj] + senders[:7]):
        pltpu.make_async_copy(slot(1 - core, j), slot(1 - core, j), bsem.at[7 + n if n else 0]).wait()
    heads = [attend(scores[h] + r_bias2[h].reshape(256, 256), vt, h) for h in range(4)]
    att = gate[...] * jnp.concatenate(heads, axis=0).T
    s_att[:, 0, :] = att
    seat = r_att.at[half, pl.ds(bj * 8 + z, 1)]

    def to_columns(g, mine):
        for px, py in gj_peers():
            for c in (1, 0):
                there = flip(c, core)
                src = s_att.at[pl.ds(there * 128 + g * 8 + px * 2 + py, 1)]
                if mine and c == 0 and py is gy and (px is gx):
                    keep(3, src, seat)
                else:
                    send(3, src, seat, {"branch": there, "gi": g, "gj": px * 2 + py})

    far_first(to_columns)
    ready("v", wv, bv)
    ready("vf", wvf, bvf)
    ready("e", we, be)
    ready("s", ws, bs)

    arrived(3, r_att)
    col = mm(split(r_att[0, :, 0, :]), weight(bf, slice(0, 128)))
    col += mm(split(r_att[1, :, 0, :]), weight(bf, slice(128, 256)))
    first[0], first[1] = col[:, :128], col[:, 128:]
    arrived(4, r_col)
    col = r_col[...].reshape(128, 256) + jnp.concatenate([first[0], first[1]], axis=1)
    xs = split(norm(col, scales[1:2, :]))
    pieces = []
    for n in range(2):
        lanes = [slice(256 * b + 128 * n, 256 * b + 128 * n + 128) for b in range(4)]
        q = split(mm(xs, weight(bv, columns=lanes[0])))
        k = split(mm(xs, weight(bv, columns=lanes[1])))
        vt = split(mm(xs, weight(bv, columns=lanes[2])).T)
        g = jax.nn.sigmoid(mm(xs, weight(bv, columns=lanes[3])))
        heads = [attend(head_scores(k, q, h), vt, h) for h in range(4)]
        pieces.append(g * jnp.concatenate(heads, axis=0).T)
    second = (
        col
        + mm(split(pieces[0]), weight(bvf, slice(0, 128)))
        + mm(split(pieces[1]), weight(bvf, slice(128, 256)))
    )
    wide = jax.nn.relu(mm(split(norm(second, scales[2:3, :])), weight(be)))
    al = second + mm(split(wide), weight(bs))
    s_al[0], s_al[1] = al[:, :128], al[:, 128:]
    for copy in loads["d"]:
        copy.wait()
    factors = mm(split(wd[...]), split(norm(al, scales[3:4, :])), NT)
    s_ab[...] = factors.reshape(2, 32, 128)

    each(gi_peers(), lambda g: send(6, s_ab.at[1], r_b.at[bj], cross(g)))

    @pl.when(gi == bj)
    def _():
        keep(6, s_ab.at[1], r_b.at[bj])

    @pl.when(gi != bj)
    def _():
        send(6, s_ab.at[1], r_b.at[bj], cross(gi))

    exchange(5, bj, on_bj, lambda b: s_ab.at[0], r_a.at[bj])

    exchange(7, bj, on_bj, lambda b: eight(s_al, b), eight(r_al, bj))
    ready("o", wo, bo)
    ready("t", wt, bt)
    ready("to", wto, bto)

    arrived(5, r_a)
    arrived(6, r_b)

    def outer_weight(g):
        parts = [weight(bo, slice(256 * g + 128 * n, 256 * g + 128 * n + 128)) for n in range(2)]
        return tuple(jnp.concatenate([parts[0][m], parts[1][m]], axis=1) for m in range(2))

    updates = f_opm(r_a[...].reshape(512, 128), r_b[...].reshape(512, 128), outer_weight)
    for n in range(2):
        rows = slice(8 * n, 8 * n + 8)
        pf[:, rows, :] = pair[:, rows, :] + updates[n]
    xs = split(norm(pf[...].reshape(256, 128), pgains[1:2, :]))
    r = [mm(xs, weight(bt, columns=slice(128 * n, 128 * n + 128))) for n in range(5)]
    ta, tb = jax.nn.sigmoid(r[1]) * r[0], jax.nn.sigmoid(r[3]) * r[2]
    for n in range(2):
        s_ta[n] = ta[128 * n : 128 * n + 128].T
        s_tb[n] = tb[128 * n : 128 * n + 128].T
    gout[...] = jax.nn.sigmoid(r[4])

    exchange(8, bj, on_bj, lambda b: eight(s_ta, b), eight(r_ta, bj))
    exchange(9, bj, on_bj, lambda b: eight(s_tb, b), eight(r_tb, bj))

    def regroup(src, dst):
        for ih in range(2):
            for bh in range(2):
                block = jnp.stack([src[ih, pl.ds(64 * bh + c, 8, stride=8), :] for c in range(8)])
                dst[:, 8 * ih : 8 * ih + 8, 128 * bh : 128 * bh + 128] = swap_blocks(block, 3, 4)

    arrived(8, r_ta)
    regroup(r_ta, s_ba)
    exchange(10, gi, on_gi, lambda g: s_ba.at[g % 8], r_ba.at[gi])
    arrived(9, r_tb)
    regroup(r_tb, s_bb)
    keep(11, s_bb.at[z], r_bb.at[z])
    for dz in (4, 3, 5, 2, 6, 1, 7):
        other = (z + dz) % 8
        send(11, s_bb.at[other], r_bb.at[z], on_gi(half * 8 + other))
    arrived(10, r_ba)
    arrived(11, r_bb)
    x = mm(split(r_ba[...].reshape(256, 256)), split(r_bb[...].reshape(128, 256)), NT)
    x = x.reshape(16, 2, 8, 128)
    for ih in range(2):
        s_d[ih, :, 0, :] = swap_blocks(x[:, ih], 3, 4).reshape(128, 128)
    place = r_d.at[:, pl.ds(bj * 8 + z, 1)]

    def to_pairs(g, mine):
        for px, py in gj_peers():
            src = s_d.at[:, pl.ds(g * 8 + px * 2 + py, 1)]
            device = {"branch": half, "gi": g, "gj": px * 2 + py}
            if mine and py is gy and px is gx:

                @pl.when(core == half)
                def _():
                    keep(13, src, place)

                @pl.when(core != half)
                def _():
                    send(13, src, place, device)
            else:
                send(13, src, place, device)

    far_first(to_pairs)

    arrived(7, r_al)
    for row in range(8):
        for n in range(2):
            out_al[row, :, 128 * n : 128 * n + 128] = r_al[n, pl.ds(row, 16, stride=8), :]

    arrived(13, r_d)
    x = norm(jnp.concatenate([r_d[0, :, 0, :].T, r_d[1, :, 0, :].T], axis=0), pgains[2:3, :])
    y = pf[...].reshape(256, 128) + gout[...] * mm(split(x), weight(bto))
    out_pair[...] = y.reshape(16, 16, 128)

    fifteen = pl.ds(0, 15)
    for n, ref in ((1, r_bias1), (4, s_col), (5, r_a)):
        sent(n, ref.at[fifteen])
    sent(0, r_raw.at[:, fifteen])
    sent(2, r_bias2.at[:, :, pl.ds(0, 120), :])
    for n, ref in ((7, s_al), (8, s_ta), (9, s_tb)):
        sent(n, ref.at[:, pl.ds(0, 120), :])
    sent(10, r_ba.at[fifteen])
    sent(11, r_bb.at[pl.ds(0, 7)])
    sent(6, r_b.at[fifteen])
    sent(3, s_att.at[pl.ds(0, 255)])
    sent(13, s_d.at[:, pl.ds(0, 127)])

    @pl.when(core != half)
    def _():
        sent(13, s_d.at[:, pl.ds(0, 1)])

    @pl.when(gi != bj)
    def _():
        sent(6, r_b.at[pl.ds(0, 1)])


def solution(mesh):
    def vmem(*shape, dtype=F32):
        return pltpu.VMEM(shape, dtype)

    widths = (
        (256, 512), (256, 256), (256, 1024), (256, 256), (256, 1024), (1024, 256), (64, 256),
        (1024, 128), (128, 640), (128, 128),
    )
    small = ((8, 2, 8, 256), (16, 16, 128), (4, 256), (3, 128), (8, 128))
    scratch = [vmem(*w) for w in small + widths]
    scratch += [vmem(2, *w, dtype=BF16) for w in widths if w != (64, 256)] + [
        vmem(2, 8, 128), vmem(16, 8, 128), vmem(4, 2, 8, 256), vmem(4, 2, 128, 256), vmem(2, 16, 8, 256),
        vmem(256, 128), vmem(4, 256, 256),
        vmem(256, 1, 128), vmem(2, 128, 1, 128), vmem(2, 128, 128), vmem(16, 8, 256), vmem(16, 8, 256),
        vmem(2, 128, 128), vmem(2, 128, 128), vmem(2, 32, 128), vmem(16, 32, 128), vmem(16, 32, 128),
        vmem(16, 16, 128), vmem(256, 128), vmem(2, 128, 128), vmem(2, 128, 128), vmem(2, 128, 128), vmem(2, 128, 128),
        vmem(8, 16, 256), vmem(8, 16, 256), vmem(16, 16, 256), vmem(8, 16, 256),
        vmem(2, 128, 1, 128), vmem(2, 128, 1, 128),
        pltpu.SemaphoreType.DMA((19,)), pltpu.SemaphoreType.DMA((14,)), pltpu.SemaphoreType.DMA((14,)),
        pltpu.SemaphoreType.DMA((15,)),
    ]

    def per_device(*args):
        args = list(args)
        args[0] = args[0].reshape(8, 2, 8, 256)
        args[4], args[11] = args[4].T, args[11].T
        return pl.pallas_call(
            kernel,
            out_shape=(
                pltpu.VMEM((8, 16, 256), F32),
                pltpu.VMEM((16, 16, 128), F32),
            ),
            in_specs=[pl.BlockSpec(memory_space=pl.ANY)] * 15,
            out_specs=(pl.BlockSpec(memory_space=pltpu.VMEM),) * 2,
            scratch_shapes=scratch,
            compiler_params=pltpu.CompilerParams(
                collective_id=0, has_side_effects=True, vmem_limit_bytes=56 * 1024 * 1024
            ),
            name="block",
        )(*args)

    msa, pairs = P(("branch", "gj"), "gi", None), P("gi", ("branch", "gj"), None)
    return jax.shard_map(
        per_device, mesh=mesh, in_specs=(msa, pairs) + (P(),) * 13, out_specs=(msa, pairs), check_vma=False
    )
```

```python
import functools
import math

import jax
import jax.numpy as jnp
from jax import lax
from jax.experimental import pallas as pl
from jax.experimental.pallas import tpu as pltpu
from jax.sharding import PartitionSpec as P

F32, BF16 = jnp.float32, jnp.bfloat16
NN = (((1,), (0,)), ((), ()))
NT = (((1,), (1,)), ((), ()))
MESH = pl.DeviceIdType.MESH
EPS = 1e-05
ROOT = 1.0 / math.sqrt(32.0)


def roll(x, shift, axis):
    return pltpu.roll(x, shift, axis)


def split(x):
    hi = x.astype(BF16)
    return hi, (x - hi.astype(F32)).astype(BF16)


def dot(a, b, dims):
    return lax.dot_general(a, b, dims, preferred_element_type=F32)


def mm(a, b, dims=NN):
    rows = a[0].shape[0]
    both = dot(jnp.concatenate(a, axis=0), b[0], dims)
    return both[:rows] + (dot(a[0], b[1], dims) + both[rows:])


def norm(x, gain):
    centred = x - jnp.mean(x, axis=-1, keepdims=True)
    variance = jnp.mean(centred * centred, axis=-1, keepdims=True)
    return centred * lax.rsqrt(variance + EPS) * gain


def iota(shape, dim):
    return lax.broadcasted_iota(jnp.int32, shape, dim)


def swap_blocks(x, bits, lane_shift):
    sub, lane = iota(x.shape, 1), iota(x.shape, 2)
    for b in range(bits):
        rows, lanes = 1 << b, 1 << (lane_shift + b)
        sbit, lbit = (sub >> b) & 1, (lane >> (lane_shift + b)) & 1
        down = roll(roll(x, lanes, 2), 8 - rows, 1)
        up = roll(roll(x, 128 - lanes, 2), rows, 1)
        x = jnp.where(sbit == lbit, x, jnp.where(sbit == 0, down, up))
    return x


def f_bias(pair, gain, wbt):
    lane, row = iota((256, 8), 0), iota((256, 8), 1)
    wide = (4 * (lane // 128) + lane // 16 % 4 == row).astype(BF16)
    w = tuple(dot(wide, part, NN).astype(BF16) for part in split(wbt))
    y = mm(split(norm(pair, gain)), w, NT)
    row, lane = iota(y.shape, 0), iota(y.shape, 1)
    own = jnp.logical_and(row % 16 == lane % 16, row // 128 == lane // 64 % 2)
    y = jnp.sum(jnp.where(own, y, 0.0).reshape(2, 8, 16, 256), axis=2)
    return y[0] + y[1]


def head_scores(k, q, h):
    own = iota(k[0].shape, 1) // 32 == h
    zero = jnp.zeros_like(k[0])
    return mm((jnp.where(own, k[0], zero), jnp.where(own, k[1], zero)), q, NT) * ROOT


def attend(scores, vt, h):
    weights = jnp.exp(scores - jnp.max(scores, axis=0, keepdims=True))
    total = jnp.sum(weights, axis=0, keepdims=True)
    rows = slice(32 * h, 32 * h + 32)
    return mm((vt[0][rows], vt[1][rows]), split(weights)) / total


def f_opm(left, right, wo):
    outer = (mm(split(left), split(right), NT) * (1.0 / 128.0)).reshape(16, 4, 8, 512)
    total = None
    for g in range(4):
        parts = [
            swap_blocks(outer[:, g, :, 128 * n : 128 * n + 128], 2, 5).reshape(128, 128)
            for n in range(4)
        ]
        term = mm(split(jnp.concatenate(parts, axis=0)), wo(g))
        total = term if total is None else total + term
    total = total.reshape(4, 16, 8, 256)
    halves = []
    for n in range(2):
        a, b = total[2 * n], total[2 * n + 1]
        even = a[..., :128] + roll(a[..., 128:], 4, 1)
        odd = b[..., 128:] + roll(b[..., :128], 4, 1)
        halves.append(jnp.where(iota(even.shape, 1) < 4, even, odd))
    return halves


def kernel(
    h_hom, h_pair, h_scales, h_pgains, h_wb, h_wq, h_wf, h_wv, h_wvf, h_we, h_ws, h_wd, h_wo, h_wt, h_wto,
    out_al, out_pair,
    hom, pair, scales, pgains, wb,
    wq, wf, wv, wvf, we, ws, wd, wo, wt, wto,
    bq, bf, bv, bvf, be, bs, bo, bt, bto,
    s_bias1, r_bias1, s_bias2, r_bias2, r_raw, gate, scores,
    s_att, r_att, first, s_col, r_col, s_al, r_al, s_ab, r_a, r_b,
    pf, gout, s_ta, s_tb, r_ta, r_tb, s_ba, s_bb, r_ba, r_bb, s_d, r_d,
    wsem, ssem, rsem, bsem, csem,
):
    core, gi, gj = lax.axis_index("branch"), lax.axis_index("gi"), lax.axis_index("gj")
    bj = core * 8 + gj
    half, z = gi // 8, gi % 8

    def on_gi(g):
        return {"gi": g}

    def on_bj(b):
        return {"branch": b // 8, "gj": b % 8}

    def cross(g):
        return {"gi": g, "branch": gi // 8, "gj": gi % 8}

    gx, gy = gj // 2, gj % 2

    def flip(bit, where):
        return where if bit == 0 else 1 - where

    def gi_peers():
        steps = sorted(((dy, dz) for dy in range(2) for dz in range(8)), key=lambda s: -2 * s[0] - min(s[1], 8 - s[1]))
        return [flip(dy, half) * 8 + (z + dz) % 8 for dy, dz in steps[:-1]]

    def gj_peers():
        steps = sorted(((dx, dy) for dx in range(4) for dy in range(2)), key=lambda s: -s[1] - min(s[0], 4 - s[0]))
        return [((gx + dx) % 4 if dx else gx, flip(dy, gy)) for dx, dy in steps]

    def bj_peers():
        own = gj_peers()
        every = [flip(dc, core) * 8 + px * 2 + py for px, py in own for dc in (1, 0)]
        return every[:-1]

    def each(peers, one):
        for peer in peers:
            one(peer)

    barrier = pltpu.get_barrier_semaphore()

    def greet(device):
        pl.semaphore_signal(barrier, inc=1, device_id=device, device_id_type=MESH)

    each(gi_peers(), lambda g: greet(on_gi(g)))
    each(bj_peers(), lambda b: greet(on_bj(b)))

    def load(n, src, dst):
        copy = pltpu.make_async_copy(src, dst, wsem.at[n])
        copy.start()
        return copy

    loads = {}
    for n, (name, src, dst) in enumerate(
        (
            ("pair", h_pair, pair), ("pgains", h_pgains, pgains), ("b", h_wb, wb),
            ("hom", h_hom, hom), ("scales", h_scales, scales),
        )
    ):
        loads[name] = load(14 + n, src, dst)

    loads["q"] = []
    for b in range(4):
        column = pl.multiple_of(256 * b + 128 * half, 128)
        loads["q"].append(load(b, h_wq.at[:, pl.ds(column, 128)], wq.at[:, pl.ds(128 * b, 128)]))
    for n, (name, src, dst) in enumerate(
        (
            ("f", h_wf, wf), ("v", h_wv, wv), ("vf", h_wvf, wvf), ("e", h_we, we), ("s", h_ws, ws),
            ("d", h_wd, wd), ("o", h_wo, wo), ("t", h_wt, wt), ("to", h_wto, wto),
        )
    ):
        loads[name] = [load(4 + n, src, dst)]

    def ready(name, src, dst):
        for copy in loads[name]:
            copy.wait()
        depth = src.shape[0]

        @pl.loop(0, depth // 32)
        def _(n):
            rows = pl.ds(pl.multiple_of(n * 32, 32), 32)
            hi, lo = split(src[rows, :])
            dst[0, rows, :] = hi
            dst[1, rows, :] = lo

    def weight(ref, rows=slice(None), columns=slice(None)):
        return ref[0, rows, columns], ref[1, rows, columns]

    def send(n, src, dst, device):
        pltpu.make_async_remote_copy(
            src_ref=src, dst_ref=dst, send_sem=ssem.at[n], recv_sem=rsem.at[n],
            device_id=device, device_id_type=MESH,
        ).start()

    def keep(n, src, dst):
        pltpu.make_async_copy(src, dst, rsem.at[n]).start()

    def exchange(n, me, device, src, dst):
        peers = gi_peers() if device is on_gi else bj_peers()
        each(peers, lambda peer: send(n, src(peer), dst, device(peer)))
        keep(n, src(me), dst)

    def far_first(one):
        @pl.loop(0, 7)
        def _(k):
            there = (z + jnp.where(k % 2 == 1, 4 - (k + 1) // 2, 4 + k // 2)) % 8
            one((1 - half) * 8 + there, False)
            one(half * 8 + there, False)

        one((1 - half) * 8 + z, False)
        one(gi, True)

    def eight(ref, b):
        return ref.at[:, pl.ds(pl.multiple_of(b * 8, 8), 8), :]

    def arrived(n, whole):
        pltpu.make_async_copy(whole, whole, rsem.at[n]).wait()

    def sent(n, most):
        pltpu.make_async_copy(most, most, ssem.at[n]).wait()

    for name in ("pair", "pgains", "b"):
        loads[name].wait()
    bias = f_bias(pair[...].reshape(256, 128), pgains[0:1, :], wb[...])
    s_bias1[0], s_bias1[1] = bias[:, :128], bias[:, 128:]
    pl.semaphore_wait(barrier, 30)
    exchange(1, gi, on_gi, lambda g: s_bias1.at[g // 8], r_bias1.at[gi])
    loads["hom"].wait()
    exchange(0, gi, on_gi, lambda g: hom.at[g % 8], r_raw.at[:, gi])
    ready("q", wq, bq)
    value = hom[...].reshape(128, 256)
    for n in range(2):
        lanes = slice(128 * n, 128 * n + 128)
        first[n] = value[:, lanes]
        for p in range(16):
            s_col[p, :, lanes] = first[n, pl.ds(p, 8, stride=16), :]
    arrived(1, r_bias1)
    turned = r_bias1[...].reshape(128, 128).T
    for ih in range(2):
        s_bias2[:, :, :, 128 * ih : 128 * ih + 128] = turned[64 * ih : 64 * ih + 64].reshape(4, 2, 8, 128)

    def slot(branch, j):
        return r_bias2.at[:, :, pl.ds(pl.multiple_of(branch * 64 + j * 8, 8), 8), :]

    def pass_on(n, src, j, device):
        pltpu.make_async_remote_copy(
            src_ref=src, dst_ref=slot(core, j), send_sem=ssem.at[2], recv_sem=bsem.at[n],
            device_id=device, device_id_type=MESH,
        ).start()

    sibling = {"branch": 1 - core}

    to = [(px * 2 + py) for px, py in gj_peers()]
    steps = sorted(((dx, dy) for dx in range(4) for dy in range(2)), key=lambda s: -s[1] - min(s[0], 4 - s[0]))
    senders = [((gx + 4 - dx) % 4 * 2 + flip(dy, gy)) for dx, dy in steps]
    for d in range(7):
        pass_on(d + 1, s_bias2, gj, {"gj": to[d]})
    pass_on(0, s_bias2, gj, sibling)
    keep(2, s_bias2, slot(core, gj))
    for d in range(7):
        j = senders[d]
        pltpu.make_async_copy(slot(core, j), slot(core, j), bsem.at[d + 1]).wait()
        pass_on(8 + d, slot(core, j), j, sibling)

    exchange(4, bj, on_bj, lambda b: s_col.at[b], r_col.at[bj])

    arrived(0, r_raw)
    loads["scales"].wait()
    x = norm(r_raw[...].reshape(256, 256), scales[0:1, :])
    xs = split(x)
    q = split(mm(xs, weight(bq, columns=slice(0, 128))))
    k = split(mm(xs, weight(bq, columns=slice(128, 256))))
    vt = split(mm(xs, weight(bq, columns=slice(256, 384))).T)
    gate[...] = jax.nn.sigmoid(mm(xs, weight(bq, columns=slice(384, 512))))
    for h in range(4):
        scores[h] = head_scores(k, q, h)
    ready("f", wf, bf)
    arrived(2, s_bias2)
    for n, j in enumerate([gj] + senders[:7]):
        pltpu.make_async_copy(slot(1 - core, j), slot(1 - core, j), bsem.at[7 + n if n else 0]).wait()
    heads = [attend(scores[h] + r_bias2[h].reshape(256, 256), vt, h) for h in range(4)]
    att = gate[...] * jnp.concatenate(heads, axis=0).T
    s_att[:, 0, :] = att
    seat = r_att.at[half, pl.ds(bj * 8 + z, 1)]

    def to_columns(g, mine):
        for px, py in gj_peers():
            for c in (1, 0):
                there = flip(c, core)
                src = s_att.at[pl.ds(there * 128 + g * 8 + px * 2 + py, 1)]
                if mine and c == 0 and py is gy and (px is gx):
                    keep(3, src, seat)
                else:
                    send(3, src, seat, {"branch": there, "gi": g, "gj": px * 2 + py})

    far_first(to_columns)
    ready("v", wv, bv)
    ready("vf", wvf, bvf)
    ready("e", we, be)
    ready("s", ws, bs)

    arrived(3, r_att)
    col = mm(split(r_att[0, :, 0, :]), weight(bf, slice(0, 128)))
    col += mm(split(r_att[1, :, 0, :]), weight(bf, slice(128, 256)))
    first[0], first[1] = col[:, :128], col[:, 128:]
    arrived(4, r_col)
    col = r_col[...].reshape(128, 256) + jnp.concatenate([first[0], first[1]], axis=1)
    xs = split(norm(col, scales[1:2, :]))
    pieces = []
    for n in range(2):
        lanes = [slice(256 * b + 128 * n, 256 * b + 128 * n + 128) for b in range(4)]
        q = split(mm(xs, weight(bv, columns=lanes[0])))
        k = split(mm(xs, weight(bv, columns=lanes[1])))
        vt = split(mm(xs, weight(bv, columns=lanes[2])).T)
        g = jax.nn.sigmoid(mm(xs, weight(bv, columns=lanes[3])))
        heads = [attend(head_scores(k, q, h), vt, h) for h in range(4)]
        pieces.append(g * jnp.concatenate(heads, axis=0).T)
    second = (
        col
        + mm(split(pieces[0]), weight(bvf, slice(0, 128)))
        + mm(split(pieces[1]), weight(bvf, slice(128, 256)))
    )
    wide = jax.nn.relu(mm(split(norm(second, scales[2:3, :])), weight(be)))
    al = second + mm(split(wide), weight(bs))
    s_al[0], s_al[1] = al[:, :128], al[:, 128:]
    for copy in loads["d"]:
        copy.wait()
    factors = mm(split(wd[...]), split(norm(al, scales[3:4, :])), NT)
    s_ab[...] = factors.reshape(2, 32, 128)

    each(gi_peers(), lambda g: send(6, s_ab.at[1], r_b.at[bj], cross(g)))

    @pl.when(gi == bj)
    def _():
        keep(6, s_ab.at[1], r_b.at[bj])

    @pl.when(gi != bj)
    def _():
        send(6, s_ab.at[1], r_b.at[bj], cross(gi))

    exchange(5, bj, on_bj, lambda b: s_ab.at[0], r_a.at[bj])

    exchange(7, bj, on_bj, lambda b: eight(s_al, b), eight(r_al, bj))
    ready("o", wo, bo)
    ready("t", wt, bt)
    ready("to", wto, bto)

    arrived(5, r_a)
    arrived(6, r_b)

    def outer_weight(g):
        parts = [weight(bo, slice(256 * g + 128 * n, 256 * g + 128 * n + 128)) for n in range(2)]
        return tuple(jnp.concatenate([parts[0][m], parts[1][m]], axis=1) for m in range(2))

    updates = f_opm(r_a[...].reshape(512, 128), r_b[...].reshape(512, 128), outer_weight)
    for n in range(2):
        rows = slice(8 * n, 8 * n + 8)
        pf[:, rows, :] = pair[:, rows, :] + updates[n]
    xs = split(norm(pf[...].reshape(256, 128), pgains[1:2, :]))
    r = [mm(xs, weight(bt, columns=slice(128 * n, 128 * n + 128))) for n in range(5)]
    ta, tb = jax.nn.sigmoid(r[1]) * r[0], jax.nn.sigmoid(r[3]) * r[2]
    for n in range(2):
        s_ta[n] = ta[128 * n : 128 * n + 128].T
        s_tb[n] = tb[128 * n : 128 * n + 128].T
    gout[...] = jax.nn.sigmoid(r[4])

    exchange(8, bj, on_bj, lambda b: eight(s_ta, b), eight(r_ta, bj))
    exchange(9, bj, on_bj, lambda b: eight(s_tb, b), eight(r_tb, bj))

    def regroup(src, dst):
        for ih in range(2):
            for bh in range(2):
                block = jnp.stack([src[ih, pl.ds(64 * bh + c, 8, stride=8), :] for c in range(8)])
                dst[:, 8 * ih : 8 * ih + 8, 128 * bh : 128 * bh + 128] = swap_blocks(block, 3, 4)

    paired = core == half

    def to_channels(one):
        for dz in (4, 3, 5, 2, 6, 1, 7):
            one((z + dz) % 8)

        @pl.when(core != half)
        def _():
            one(z)

    def left(there):
        pltpu.make_async_remote_copy(
            src_ref=s_ba.at[there], dst_ref=r_ba.at[gi], send_sem=ssem.at[10], recv_sem=csem.at[gi],
            device_id={"gi": core * 8 + there}, device_id_type=MESH,
        ).start()

    def right(there):
        send(11, s_bb.at[there], r_bb.at[z], {"gi": core * 8 + there, "branch": half})

    arrived(8, r_ta)
    regroup(r_ta, s_ba)
    to_channels(left)

    @pl.when(paired)
    def _():
        pltpu.make_async_copy(s_ba.at[z], r_ba.at[gi], csem.at[gi]).start()

    arrived(9, r_tb)
    regroup(r_tb, s_bb)
    to_channels(right)

    @pl.when(paired)
    def _():
        keep(11, s_bb.at[z], r_bb.at[z])
        for dy in range(2):
            for dz in (0, 1, 7, 2, 6, 3, 5, 4):
                g = flip(dy, half) * 8 + (z + dz) % 8
                pltpu.make_async_copy(r_ba.at[g], r_ba.at[g], csem.at[g]).wait()
                send(10, r_ba.at[g], r_ba.at[g], sibling)

    @pl.when(jnp.logical_not(paired))
    def _():
        arrived(10, r_ba)

    arrived(11, r_bb)
    x = mm(split(r_ba[...].reshape(256, 256)), split(r_bb[...].reshape(128, 256)), NT)
    x = x.reshape(16, 2, 8, 128)
    for ih in range(2):
        s_d[ih, :, 0, :] = swap_blocks(x[:, ih], 3, 4).reshape(128, 128)
    place = r_d.at[:, pl.ds((half * 8 + gj) * 8 + z, 1)]

    def to_pairs(g, mine):
        for px, py in gj_peers():
            src = s_d.at[:, pl.ds(g * 8 + px * 2 + py, 1)]
            if mine and py is gy and px is gx:
                keep(13, src, place)
            else:
                send(13, src, place, {"gi": g, "gj": px * 2 + py})

    far_first(to_pairs)

    arrived(7, r_al)
    for row in range(8):
        for n in range(2):
            out_al[row, :, 128 * n : 128 * n + 128] = r_al[n, pl.ds(row, 16, stride=8), :]

    arrived(13, r_d)
    x = norm(jnp.concatenate([r_d[0, :, 0, :].T, r_d[1, :, 0, :].T], axis=0), pgains[2:3, :])
    y = pf[...].reshape(256, 128) + gout[...] * mm(split(x), weight(bto))
    out_pair[...] = y.reshape(16, 16, 128)

    fifteen = pl.ds(0, 15)
    for n, ref in ((1, r_bias1), (4, s_col), (5, r_a)):
        sent(n, ref.at[fifteen])
    sent(0, r_raw.at[:, fifteen])
    sent(2, r_bias2.at[:, :, pl.ds(0, 120), :])
    for n, ref in ((7, s_al), (8, s_ta), (9, s_tb)):
        sent(n, ref.at[:, pl.ds(0, 120), :])
    sent(10, r_ba.at[pl.ds(0, 7)])

    @pl.when(paired)
    def _():
        sent(10, r_ba)

    @pl.when(jnp.logical_not(paired))
    def _():
        sent(10, r_ba.at[pl.ds(0, 1)])
        sent(11, r_bb.at[pl.ds(0, 1)])

    sent(11, r_bb.at[pl.ds(0, 7)])
    sent(6, r_b.at[fifteen])
    sent(3, s_att.at[pl.ds(0, 255)])
    sent(13, s_d.at[:, pl.ds(0, 127)])

    @pl.when(gi != bj)
    def _():
        sent(6, r_b.at[pl.ds(0, 1)])


def solution(mesh):
    def vmem(*shape, dtype=F32):
        return pltpu.VMEM(shape, dtype)

    widths = (
        (256, 512), (256, 256), (256, 1024), (256, 256), (256, 1024), (1024, 256), (64, 256),
        (1024, 128), (128, 640), (128, 128),
    )
    small = ((8, 2, 8, 256), (16, 16, 128), (4, 256), (3, 128), (8, 128))
    scratch = [vmem(*w) for w in small + widths]
    scratch += [vmem(2, *w, dtype=BF16) for w in widths if w != (64, 256)] + [
        vmem(2, 8, 128), vmem(16, 8, 128), vmem(4, 2, 8, 256), vmem(4, 2, 128, 256), vmem(2, 16, 8, 256),
        vmem(256, 128), vmem(4, 256, 256),
        vmem(256, 1, 128), vmem(2, 128, 1, 128), vmem(2, 128, 128), vmem(16, 8, 256), vmem(16, 8, 256),
        vmem(2, 128, 128), vmem(2, 128, 128), vmem(2, 32, 128), vmem(16, 32, 128), vmem(16, 32, 128),
        vmem(16, 16, 128), vmem(256, 128), vmem(2, 128, 128), vmem(2, 128, 128), vmem(2, 128, 128), vmem(2, 128, 128),
        vmem(8, 16, 256), vmem(8, 16, 256), vmem(16, 16, 256), vmem(8, 16, 256),
        vmem(2, 128, 1, 128), vmem(2, 128, 1, 128),
        pltpu.SemaphoreType.DMA((19,)), pltpu.SemaphoreType.DMA((14,)), pltpu.SemaphoreType.DMA((14,)),
        pltpu.SemaphoreType.DMA((15,)), pltpu.SemaphoreType.DMA((16,)),
    ]

    def per_device(*args):
        args = list(args)
        args[0] = args[0].reshape(8, 2, 8, 256)
        args[4], args[11] = args[4].T, args[11].T
        return pl.pallas_call(
            kernel,
            out_shape=(
                pltpu.VMEM((8, 16, 256), F32),
                pltpu.VMEM((16, 16, 128), F32),
            ),
            in_specs=[pl.BlockSpec(memory_space=pl.ANY)] * 15,
            out_specs=(pl.BlockSpec(memory_space=pltpu.VMEM),) * 2,
            scratch_shapes=scratch,
            compiler_params=pltpu.CompilerParams(
                collective_id=0, has_side_effects=True, vmem_limit_bytes=56 * 1024 * 1024
            ),
            name="block",
        )(*args)

    msa, pairs = P(("branch", "gj"), "gi", None), P("gi", ("branch", "gj"), None)
    return jax.shard_map(
        per_device, mesh=mesh, in_specs=(msa, pairs) + (P(),) * 13, out_specs=(msa, pairs), check_vma=False
    )
```

```python
import functools
import math

import jax
import jax.numpy as jnp
from jax import lax
from jax.experimental import pallas as pl
from jax.experimental.pallas import tpu as pltpu
from jax.sharding import PartitionSpec as P

F32, BF16 = jnp.float32, jnp.bfloat16
NN = (((1,), (0,)), ((), ()))
NT = (((1,), (1,)), ((), ()))
MESH = pl.DeviceIdType.MESH
EPS = 1e-05
ROOT = 1.0 / math.sqrt(32.0)


def roll(x, shift, axis):
    return pltpu.roll(x, shift, axis)


def split(x):
    hi = x.astype(BF16)
    return hi, (x - hi.astype(F32)).astype(BF16)


def dot(a, b, dims):
    return lax.dot_general(a, b, dims, preferred_element_type=F32)


def mm(a, b, dims=NN):
    rows = a[0].shape[0]
    both = dot(jnp.concatenate(a, axis=0), b[0], dims)
    return both[:rows] + (dot(a[0], b[1], dims) + both[rows:])


def norm(x, gain):
    centred = x - jnp.mean(x, axis=-1, keepdims=True)
    variance = jnp.mean(centred * centred, axis=-1, keepdims=True)
    return centred * lax.rsqrt(variance + EPS) * gain


def iota(shape, dim):
    return lax.broadcasted_iota(jnp.int32, shape, dim)


def swap_blocks(x, bits, lane_shift):
    sub, lane = iota(x.shape, 1), iota(x.shape, 2)
    for b in range(bits):
        rows, lanes = 1 << b, 1 << (lane_shift + b)
        sbit, lbit = (sub >> b) & 1, (lane >> (lane_shift + b)) & 1
        down = roll(roll(x, lanes, 2), 8 - rows, 1)
        up = roll(roll(x, 128 - lanes, 2), rows, 1)
        x = jnp.where(sbit == lbit, x, jnp.where(sbit == 0, down, up))
    return x


def f_bias(pair, gain, wbt):
    lane, row = iota((256, 8), 0), iota((256, 8), 1)
    wide = (4 * (lane // 128) + lane // 16 % 4 == row).astype(BF16)
    w = tuple(dot(wide, part, NN).astype(BF16) for part in split(wbt))
    y = mm(split(norm(pair, gain)), w, NT)
    row, lane = iota(y.shape, 0), iota(y.shape, 1)
    own = jnp.logical_and(row % 16 == lane % 16, row // 128 == lane // 64 % 2)
    y = jnp.sum(jnp.where(own, y, 0.0).reshape(2, 8, 16, 256), axis=2)
    return y[0] + y[1]


def head_scores(k, q, h):
    own = iota(k[0].shape, 1) // 32 == h
    zero = jnp.zeros_like(k[0])
    return mm((jnp.where(own, k[0], zero), jnp.where(own, k[1], zero)), q, NT) * ROOT


def attend(scores, vt, h):
    weights = jnp.exp(scores - jnp.max(scores, axis=0, keepdims=True))
    total = jnp.sum(weights, axis=0, keepdims=True)
    rows = slice(32 * h, 32 * h + 32)
    return mm((vt[0][rows], vt[1][rows]), split(weights)) / total


def f_opm(left, right, wo):
    outer = (mm(split(left), split(right), NT) * (1.0 / 128.0)).reshape(16, 4, 8, 512)
    total = None
    for g in range(4):
        parts = [
            swap_blocks(outer[:, g, :, 128 * n : 128 * n + 128], 2, 5).reshape(128, 128)
            for n in range(4)
        ]
        term = mm(split(jnp.concatenate(parts, axis=0)), wo(g))
        total = term if total is None else total + term
    total = total.reshape(4, 16, 8, 256)
    halves = []
    for n in range(2):
        a, b = total[2 * n], total[2 * n + 1]
        even = a[..., :128] + roll(a[..., 128:], 4, 1)
        odd = b[..., 128:] + roll(b[..., :128], 4, 1)
        halves.append(jnp.where(iota(even.shape, 1) < 4, even, odd))
    return halves


def kernel(
    h_hom, h_pair, h_scales, h_pgains, h_wb, h_wq, h_wf, h_wv, h_wvf, h_we, h_ws, h_wd, h_wo, h_wt, h_wto,
    out_al, out_pair,
    hom, pair, scales, pgains, wb,
    wq, wf, wv, wvf, we, ws, wd, wo, wt, wto,
    bq, bf, bv, bvf, be, bs, bo, bt, bto,
    s_bias1, r_bias1, s_bias2, r_bias2, r_raw, gate, scores, turned_v,
    s_att, r_att, first, s_col, r_col, s_al, r_al, s_ab, r_a, r_b,
    pf, gout, s_ta, s_tb, r_ta, r_tb, s_ba, s_bb, r_ba, r_bb, s_d, r_d,
    wsem, ssem, rsem, bsem, csem,
):
    core, gi, gj = lax.axis_index("branch"), lax.axis_index("gi"), lax.axis_index("gj")
    bj = core * 8 + gj
    half, z = gi // 8, gi % 8

    def on_gi(g):
        return {"gi": g}

    def on_bj(b):
        return {"branch": b // 8, "gj": b % 8}

    def cross(g):
        return {"gi": g, "branch": gi // 8, "gj": gi % 8}

    gx, gy = gj // 2, gj % 2

    def flip(bit, where):
        return where if bit == 0 else 1 - where

    def gi_peers():
        steps = sorted(((dy, dz) for dy in range(2) for dz in range(8)), key=lambda s: -2 * s[0] - min(s[1], 8 - s[1]))
        return [flip(dy, half) * 8 + (z + dz) % 8 for dy, dz in steps[:-1]]

    def gj_peers():
        steps = sorted(((dx, dy) for dx in range(4) for dy in range(2)), key=lambda s: -s[1] - min(s[0], 4 - s[0]))
        return [((gx + dx) % 4 if dx else gx, flip(dy, gy)) for dx, dy in steps]

    def bj_peers():
        own = gj_peers()
        every = [flip(dc, core) * 8 + px * 2 + py for px, py in own for dc in (1, 0)]
        return every[:-1]

    def each(peers, one):
        for peer in peers:
            one(peer)

    barrier = pltpu.get_barrier_semaphore()

    def greet(device):
        pl.semaphore_signal(barrier, inc=1, device_id=device, device_id_type=MESH)

    each(gi_peers(), lambda g: greet(on_gi(g)))
    each(bj_peers(), lambda b: greet(on_bj(b)))

    def load(n, src, dst):
        copy = pltpu.make_async_copy(src, dst, wsem.at[n])
        copy.start()
        return copy

    loads = {}
    for n, (name, src, dst) in enumerate(
        (
            ("pair", h_pair, pair), ("pgains", h_pgains, pgains), ("b", h_wb, wb),
            ("hom", h_hom, hom), ("scales", h_scales, scales),
        )
    ):
        loads[name] = load(14 + n, src, dst)

    loads["q"] = []
    for b in range(4):
        column = pl.multiple_of(256 * b + 128 * half, 128)
        loads["q"].append(load(b, h_wq.at[:, pl.ds(column, 128)], wq.at[:, pl.ds(128 * b, 128)]))
    for n, (name, src, dst) in enumerate(
        (
            ("f", h_wf, wf), ("v", h_wv, wv), ("vf", h_wvf, wvf), ("e", h_we, we), ("s", h_ws, ws),
            ("d", h_wd, wd), ("o", h_wo, wo), ("t", h_wt, wt), ("to", h_wto, wto),
        )
    ):
        loads[name] = [load(4 + n, src, dst)]

    def ready(name, src, dst):
        for copy in loads[name]:
            copy.wait()
        depth = src.shape[0]

        @pl.loop(0, depth // 32)
        def _(n):
            rows = pl.ds(pl.multiple_of(n * 32, 32), 32)
            hi, lo = split(src[rows, :])
            dst[0, rows, :] = hi
            dst[1, rows, :] = lo

    def weight(ref, rows=slice(None), columns=slice(None)):
        return ref[0, rows, columns], ref[1, rows, columns]

    def send(n, src, dst, device):
        pltpu.make_async_remote_copy(
            src_ref=src, dst_ref=dst, send_sem=ssem.at[n], recv_sem=rsem.at[n],
            device_id=device, device_id_type=MESH,
        ).start()

    def keep(n, src, dst):
        pltpu.make_async_copy(src, dst, rsem.at[n]).start()

    def exchange(n, me, device, src, dst):
        peers = gi_peers() if device is on_gi else bj_peers()
        each(peers, lambda peer: send(n, src(peer), dst, device(peer)))
        keep(n, src(me), dst)

    def far_first(one):
        @pl.loop(0, 7)
        def _(k):
            there = (z + jnp.where(k % 2 == 1, 4 - (k + 1) // 2, 4 + k // 2)) % 8
            one((1 - half) * 8 + there, False)
            one(half * 8 + there, False)

        one((1 - half) * 8 + z, False)
        one(gi, True)

    def eight(ref, b):
        return ref.at[:, pl.ds(pl.multiple_of(b * 8, 8), 8), :]

    def arrived(n, whole):
        pltpu.make_async_copy(whole, whole, rsem.at[n]).wait()

    def sent(n, most):
        pltpu.make_async_copy(most, most, ssem.at[n]).wait()

    for name in ("pair", "pgains", "b"):
        loads[name].wait()
    bias = f_bias(pair[...].reshape(256, 128), pgains[0:1, :], wb[...])
    s_bias1[0], s_bias1[1] = bias[:, :128], bias[:, 128:]
    pl.semaphore_wait(barrier, 30)
    exchange(1, gi, on_gi, lambda g: s_bias1.at[g // 8], r_bias1.at[gi])
    loads["hom"].wait()
    exchange(0, gi, on_gi, lambda g: hom.at[g % 8], r_raw.at[:, gi])
    ready("q", wq, bq)
    value = hom[...].reshape(128, 256)
    for n in range(2):
        lanes = slice(128 * n, 128 * n + 128)
        first[n] = value[:, lanes]
        for p in range(16):
            s_col[p, :, lanes] = first[n, pl.ds(p, 8, stride=16), :]
    arrived(1, r_bias1)
    turned = r_bias1[...].reshape(128, 128).T
    for ih in range(2):
        s_bias2[:, :, :, 128 * ih : 128 * ih + 128] = turned[64 * ih : 64 * ih + 64].reshape(4, 2, 8, 128)

    def slot(branch, j):
        return r_bias2.at[:, :, pl.ds(pl.multiple_of(branch * 64 + j * 8, 8), 8), :]

    def pass_on(n, src, j, device):
        pltpu.make_async_remote_copy(
            src_ref=src, dst_ref=slot(core, j), send_sem=ssem.at[2], recv_sem=bsem.at[n],
            device_id=device, device_id_type=MESH,
        ).start()

    sibling = {"branch": 1 - core}

    to = [(px * 2 + py) for px, py in gj_peers()]
    steps = sorted(((dx, dy) for dx in range(4) for dy in range(2)), key=lambda s: -s[1] - min(s[0], 4 - s[0]))
    senders = [((gx + 4 - dx) % 4 * 2 + flip(dy, gy)) for dx, dy in steps]
    for d in range(7):
        pass_on(d + 1, s_bias2, gj, {"gj": to[d]})
    pass_on(0, s_bias2, gj, sibling)
    keep(2, s_bias2, slot(core, gj))
    arrived(0, r_raw)
    loads["scales"].wait()
    x = norm(r_raw[...].reshape(256, 256), scales[0:1, :])
    p = mm(split(x), weight(bq))
    q, k, vt = split(p[:, :128]), split(p[:, 128:256]), split(p[:, 256:384].T)
    gate[...] = jax.nn.sigmoid(p[:, 384:])
    for h in range(4):
        scores[h] = head_scores(k, q, h)
    turned_v[0], turned_v[1] = vt

    for d in range(7):
        j = senders[d]
        pltpu.make_async_copy(slot(core, j), slot(core, j), bsem.at[d + 1]).wait()
        pass_on(8 + d, slot(core, j), j, sibling)

    exchange(4, bj, on_bj, lambda b: s_col.at[b], r_col.at[bj])
    ready("f", wf, bf)
    arrived(2, s_bias2)
    for n, j in enumerate([gj] + senders[:7]):
        pltpu.make_async_copy(slot(1 - core, j), slot(1 - core, j), bsem.at[7 + n if n else 0]).wait()
    vt = turned_v[0], turned_v[1]
    heads = [attend(scores[h] + r_bias2[h].reshape(256, 256), vt, h) for h in range(4)]
    att = gate[...] * jnp.concatenate(heads, axis=0).T
    s_att[:, 0, :] = att
    seat = r_att.at[half, pl.ds(bj * 8 + z, 1)]

    def to_columns(g, mine):
        for px, py in gj_peers():
            for c in (1, 0):
                there = flip(c, core)
                src = s_att.at[pl.ds(there * 128 + g * 8 + px * 2 + py, 1)]
                if mine and c == 0 and py is gy and (px is gx):
                    keep(3, src, seat)
                else:
                    send(3, src, seat, {"branch": there, "gi": g, "gj": px * 2 + py})

    far_first(to_columns)
    ready("v", wv, bv)
    ready("vf", wvf, bvf)
    ready("e", we, be)
    ready("s", ws, bs)

    arrived(3, r_att)
    col = mm(split(r_att[0, :, 0, :]), weight(bf, slice(0, 128)))
    col += mm(split(r_att[1, :, 0, :]), weight(bf, slice(128, 256)))
    first[0], first[1] = col[:, :128], col[:, 128:]
    arrived(4, r_col)
    col = r_col[...].reshape(128, 256) + jnp.concatenate([first[0], first[1]], axis=1)
    xs = split(norm(col, scales[1:2, :]))
    p = mm(xs, weight(bv))
    pieces = []
    for n in range(2):
        q, k, v, g = (p[:, 256 * b + 128 * n : 256 * b + 128 * n + 128] for b in range(4))
        q, k, vt, g = split(q), split(k), split(v.T), jax.nn.sigmoid(g)
        heads = [attend(head_scores(k, q, h), vt, h) for h in range(4)]
        pieces.append(g * jnp.concatenate(heads, axis=0).T)
    second = (
        col
        + mm(split(pieces[0]), weight(bvf, slice(0, 128)))
        + mm(split(pieces[1]), weight(bvf, slice(128, 256)))
    )
    wide = jax.nn.relu(mm(split(norm(second, scales[2:3, :])), weight(be)))
    al = second + mm(split(wide), weight(bs))
    s_al[0], s_al[1] = al[:, :128], al[:, 128:]
    for copy in loads["d"]:
        copy.wait()
    factors = mm(split(wd[...]), split(norm(al, scales[3:4, :])), NT)
    s_ab[...] = factors.reshape(2, 32, 128)

    each(gi_peers(), lambda g: send(6, s_ab.at[1], r_b.at[bj], cross(g)))

    @pl.when(gi == bj)
    def _():
        keep(6, s_ab.at[1], r_b.at[bj])

    @pl.when(gi != bj)
    def _():
        send(6, s_ab.at[1], r_b.at[bj], cross(gi))

    exchange(5, bj, on_bj, lambda b: s_ab.at[0], r_a.at[bj])

    exchange(7, bj, on_bj, lambda b: eight(s_al, b), eight(r_al, bj))
    ready("o", wo, bo)
    ready("t", wt, bt)
    ready("to", wto, bto)

    arrived(5, r_a)
    arrived(6, r_b)

    def outer_weight(g):
        parts = [weight(bo, slice(256 * g + 128 * n, 256 * g + 128 * n + 128)) for n in range(2)]
        return tuple(jnp.concatenate([parts[0][m], parts[1][m]], axis=1) for m in range(2))

    updates = f_opm(r_a[...].reshape(512, 128), r_b[...].reshape(512, 128), outer_weight)
    for n in range(2):
        rows = slice(8 * n, 8 * n + 8)
        pf[:, rows, :] = pair[:, rows, :] + updates[n]
    xs = split(norm(pf[...].reshape(256, 128), pgains[1:2, :]))
    p = mm(xs, weight(bt))
    r = [p[:, 128 * n : 128 * n + 128] for n in range(5)]
    ta, tb = jax.nn.sigmoid(r[1]) * r[0], jax.nn.sigmoid(r[3]) * r[2]
    for n in range(2):
        s_ta[n] = ta[128 * n : 128 * n + 128].T
        s_tb[n] = tb[128 * n : 128 * n + 128].T
    gout[...] = jax.nn.sigmoid(r[4])

    exchange(8, bj, on_bj, lambda b: eight(s_ta, b), eight(r_ta, bj))
    exchange(9, bj, on_bj, lambda b: eight(s_tb, b), eight(r_tb, bj))

    def regroup(src, dst):
        for ih in range(2):
            for bh in range(2):
                block = jnp.stack([src[ih, pl.ds(64 * bh + c, 8, stride=8), :] for c in range(8)])
                dst[:, 8 * ih : 8 * ih + 8, 128 * bh : 128 * bh + 128] = swap_blocks(block, 3, 4)

    paired = core == half

    def to_channels(one):
        for dz in (4, 3, 5, 2, 6, 1, 7):
            one((z + dz) % 8)

        @pl.when(core != half)
        def _():
            one(z)

    def left(there):
        pltpu.make_async_remote_copy(
            src_ref=s_ba.at[there], dst_ref=r_ba.at[gi], send_sem=ssem.at[10], recv_sem=csem.at[gi],
            device_id={"gi": core * 8 + there}, device_id_type=MESH,
        ).start()

    def right(there):
        send(11, s_bb.at[there], r_bb.at[z], {"gi": core * 8 + there, "branch": half})

    arrived(8, r_ta)
    regroup(r_ta, s_ba)
    to_channels(left)

    @pl.when(paired)
    def _():
        pltpu.make_async_copy(s_ba.at[z], r_ba.at[gi], csem.at[gi]).start()

    arrived(9, r_tb)
    regroup(r_tb, s_bb)
    to_channels(right)

    @pl.when(paired)
    def _():
        keep(11, s_bb.at[z], r_bb.at[z])
        for dy in range(2):
            for dz in (0, 1, 7, 2, 6, 3, 5, 4):
                g = flip(dy, half) * 8 + (z + dz) % 8
                pltpu.make_async_copy(r_ba.at[g], r_ba.at[g], csem.at[g]).wait()
                send(10, r_ba.at[g], r_ba.at[g], sibling)

    @pl.when(jnp.logical_not(paired))
    def _():
        arrived(10, r_ba)

    arrived(11, r_bb)
    x = mm(split(r_ba[...].reshape(256, 256)), split(r_bb[...].reshape(128, 256)), NT)
    x = x.reshape(16, 2, 8, 128)
    for ih in range(2):
        s_d[ih, :, 0, :] = swap_blocks(x[:, ih], 3, 4).reshape(128, 128)
    place = r_d.at[:, pl.ds((half * 8 + gj) * 8 + z, 1)]

    def to_pairs(g, mine):
        for px, py in gj_peers():
            src = s_d.at[:, pl.ds(g * 8 + px * 2 + py, 1)]
            if mine and py is gy and px is gx:
                keep(13, src, place)
            else:
                send(13, src, place, {"gi": g, "gj": px * 2 + py})

    far_first(to_pairs)

    arrived(7, r_al)
    for row in range(8):
        for n in range(2):
            out_al[row, :, 128 * n : 128 * n + 128] = r_al[n, pl.ds(row, 16, stride=8), :]

    arrived(13, r_d)
    x = norm(jnp.concatenate([r_d[0, :, 0, :].T, r_d[1, :, 0, :].T], axis=0), pgains[2:3, :])
    y = pf[...].reshape(256, 128) + gout[...] * mm(split(x), weight(bto))
    out_pair[...] = y.reshape(16, 16, 128)

    fifteen = pl.ds(0, 15)
    for n, ref in ((1, r_bias1), (4, s_col), (5, r_a)):
        sent(n, ref.at[fifteen])
    sent(0, r_raw.at[:, fifteen])
    sent(2, r_bias2.at[:, :, pl.ds(0, 120), :])
    for n, ref in ((7, s_al), (8, s_ta), (9, s_tb)):
        sent(n, ref.at[:, pl.ds(0, 120), :])
    sent(10, r_ba.at[pl.ds(0, 7)])

    @pl.when(paired)
    def _():
        sent(10, r_ba)

    @pl.when(jnp.logical_not(paired))
    def _():
        sent(10, r_ba.at[pl.ds(0, 1)])
        sent(11, r_bb.at[pl.ds(0, 1)])

    sent(11, r_bb.at[pl.ds(0, 7)])
    sent(6, r_b.at[fifteen])
    sent(3, s_att.at[pl.ds(0, 255)])
    sent(13, s_d.at[:, pl.ds(0, 127)])

    @pl.when(gi != bj)
    def _():
        sent(6, r_b.at[pl.ds(0, 1)])


def solution(mesh):
    def vmem(*shape, dtype=F32):
        return pltpu.VMEM(shape, dtype)

    widths = (
        (256, 512), (256, 256), (256, 1024), (256, 256), (256, 1024), (1024, 256), (64, 256),
        (1024, 128), (128, 640), (128, 128),
    )
    small = ((8, 2, 8, 256), (16, 16, 128), (4, 256), (3, 128), (8, 128))
    scratch = [vmem(*w) for w in small + widths]
    scratch += [vmem(2, *w, dtype=BF16) for w in widths if w != (64, 256)] + [
        vmem(2, 8, 128), vmem(16, 8, 128), vmem(4, 2, 8, 256), vmem(4, 2, 128, 256), vmem(2, 16, 8, 256),
        vmem(256, 128), vmem(4, 256, 256), vmem(2, 128, 256, dtype=BF16),
        vmem(256, 1, 128), vmem(2, 128, 1, 128), vmem(2, 128, 128), vmem(16, 8, 256), vmem(16, 8, 256),
        vmem(2, 128, 128), vmem(2, 128, 128), vmem(2, 32, 128), vmem(16, 32, 128), vmem(16, 32, 128),
        vmem(16, 16, 128), vmem(256, 128), vmem(2, 128, 128), vmem(2, 128, 128), vmem(2, 128, 128), vmem(2, 128, 128),
        vmem(8, 16, 256), vmem(8, 16, 256), vmem(16, 16, 256), vmem(8, 16, 256),
        vmem(2, 128, 1, 128), vmem(2, 128, 1, 128),
        pltpu.SemaphoreType.DMA((19,)), pltpu.SemaphoreType.DMA((14,)), pltpu.SemaphoreType.DMA((14,)),
        pltpu.SemaphoreType.DMA((15,)), pltpu.SemaphoreType.DMA((16,)),
    ]

    def per_device(*args):
        args = list(args)
        args[0] = args[0].reshape(8, 2, 8, 256)
        args[4], args[11] = args[4].T, args[11].T
        return pl.pallas_call(
            kernel,
            out_shape=(
                pltpu.VMEM((8, 16, 256), F32),
                pltpu.VMEM((16, 16, 128), F32),
            ),
            in_specs=[pl.BlockSpec(memory_space=pl.ANY)] * 15,
            out_specs=(pl.BlockSpec(memory_space=pltpu.VMEM),) * 2,
            scratch_shapes=scratch,
            compiler_params=pltpu.CompilerParams(
                collective_id=0, has_side_effects=True, vmem_limit_bytes=56 * 1024 * 1024
            ),
            name="block",
        )(*args)

    msa, pairs = P(("branch", "gj"), "gi", None), P("gi", ("branch", "gj"), None)
    return jax.shard_map(
        per_device, mesh=mesh, in_specs=(msa, pairs) + (P(),) * 13, out_specs=(msa, pairs), check_vma=False
    )
```

```python
import functools
import math

import jax
import jax.numpy as jnp
from jax import lax
from jax.experimental import pallas as pl
from jax.experimental.pallas import tpu as pltpu
from jax.sharding import PartitionSpec as P

F32, BF16 = jnp.float32, jnp.bfloat16
NN = (((1,), (0,)), ((), ()))
NT = (((1,), (1,)), ((), ()))
MESH = pl.DeviceIdType.MESH
EPS = 1e-05
ROOT = 1.0 / math.sqrt(32.0)


def roll(x, shift, axis):
    return pltpu.roll(x, shift, axis)


def split(x):
    hi = x.astype(BF16)
    return hi, (x - hi.astype(F32)).astype(BF16)


def dot(a, b, dims):
    return lax.dot_general(a, b, dims, preferred_element_type=F32)


def mm(a, b, dims=NN):
    rows = a[0].shape[0]
    both = dot(jnp.concatenate(a, axis=0), b[0], dims)
    return both[:rows] + (dot(a[0], b[1], dims) + both[rows:])


def norm(x, gain):
    centred = x - jnp.mean(x, axis=-1, keepdims=True)
    variance = jnp.mean(centred * centred, axis=-1, keepdims=True)
    return centred * lax.rsqrt(variance + EPS) * gain


def iota(shape, dim):
    return lax.broadcasted_iota(jnp.int32, shape, dim)


def swap_blocks(x, bits, lane_shift):
    sub, lane = iota(x.shape, 1), iota(x.shape, 2)
    for b in range(bits):
        rows, lanes = 1 << b, 1 << (lane_shift + b)
        sbit, lbit = (sub >> b) & 1, (lane >> (lane_shift + b)) & 1
        down = roll(roll(x, lanes, 2), 8 - rows, 1)
        up = roll(roll(x, 128 - lanes, 2), rows, 1)
        x = jnp.where(sbit == lbit, x, jnp.where(sbit == 0, down, up))
    return x


def f_bias(pair, gain, wbt):
    lane, row = iota((256, 8), 0), iota((256, 8), 1)
    wide = (4 * (lane // 128) + lane // 16 % 4 == row).astype(BF16)
    w = tuple(dot(wide, part, NN).astype(BF16) for part in split(wbt))
    y = mm(split(norm(pair, gain)), w, NT)
    row, lane = iota(y.shape, 0), iota(y.shape, 1)
    own = jnp.logical_and(row % 16 == lane % 16, row // 128 == lane // 64 % 2)
    y = jnp.sum(jnp.where(own, y, 0.0).reshape(2, 8, 16, 256), axis=2)
    return y[0] + y[1]


def head_scores(k, q, h):
    own = iota(k[0].shape, 1) // 32 == h
    zero = jnp.zeros_like(k[0])
    return mm((jnp.where(own, k[0], zero), jnp.where(own, k[1], zero)), q, NT) * ROOT


def attend(scores, vt, h):
    weights = jnp.exp(scores - jnp.max(scores, axis=0, keepdims=True))
    total = jnp.sum(weights, axis=0, keepdims=True)
    rows = slice(32 * h, 32 * h + 32)
    return mm((vt[0][rows], vt[1][rows]), split(weights)) / total


def f_opm(left, right, wo):
    outer = (mm(split(left), split(right), NT) * (1.0 / 128.0)).reshape(16, 4, 8, 512)
    total = None
    for g in range(4):
        parts = [
            swap_blocks(outer[:, g, :, 128 * n : 128 * n + 128], 2, 5).reshape(128, 128)
            for n in range(4)
        ]
        term = mm(split(jnp.concatenate(parts, axis=0)), wo(g))
        total = term if total is None else total + term
    total = total.reshape(4, 16, 8, 256)
    halves = []
    for n in range(2):
        a, b = total[2 * n], total[2 * n + 1]
        even = a[..., :128] + roll(a[..., 128:], 4, 1)
        odd = b[..., 128:] + roll(b[..., :128], 4, 1)
        halves.append(jnp.where(iota(even.shape, 1) < 4, even, odd))
    return halves


def kernel(
    h_hom, h_pair, h_scales, h_pgains, h_wb, h_wq, h_wf, h_wv, h_wvf, h_we, h_ws, h_wd, h_wo, h_wt, h_wto,
    out_al, out_pair,
    hom, pair, scales, pgains, wb,
    wq, wf, wv, wvf, we, ws, wd, wo, wt, wto,
    bq, bf, bv, bvf, be, bs, bo, bt, bto,
    s_bias1, r_bias1, s_bias2, r_bias2, r_raw, gate, scores, turned_v,
    s_att, r_att, first, s_col, r_col, s_al, r_al, s_ab, r_a, r_b,
    pf, gout, s_ta, s_tb, r_ta, r_tb, s_ba, s_bb, r_ba, r_bb, s_d, r_d,
    wsem, ssem, rsem, bsem, csem,
):
    core, gi, gj = lax.axis_index("branch"), lax.axis_index("gi"), lax.axis_index("gj")
    bj = core * 8 + gj
    half, z = gi // 8, gi % 8

    def on_gi(g):
        return {"gi": g}

    def on_bj(b):
        return {"branch": b // 8, "gj": b % 8}

    def cross(g):
        return {"gi": g, "branch": gi // 8, "gj": gi % 8}

    gx, gy = gj // 2, gj % 2

    def flip(bit, where):
        return where if bit == 0 else 1 - where

    def gi_peers():
        steps = sorted(((dy, dz) for dy in range(2) for dz in range(8)), key=lambda s: -2 * s[0] - min(s[1], 8 - s[1]))
        return [flip(dy, half) * 8 + (z + dz) % 8 for dy, dz in steps[:-1]]

    def gj_peers():
        steps = sorted(((dx, dy) for dx in range(4) for dy in range(2)), key=lambda s: -s[1] - min(s[0], 4 - s[0]))
        return [((gx + dx) % 4 if dx else gx, flip(dy, gy)) for dx, dy in steps]

    def bj_peers():
        own = gj_peers()
        every = [flip(dc, core) * 8 + px * 2 + py for px, py in own for dc in (1, 0)]
        return every[:-1]

    def each(peers, one):
        for peer in peers:
            one(peer)

    barrier = pltpu.get_barrier_semaphore()

    def greet(device):
        pl.semaphore_signal(barrier, inc=1, device_id=device, device_id_type=MESH)

    each(gi_peers(), lambda g: greet(on_gi(g)))
    each(bj_peers(), lambda b: greet(on_bj(b)))

    def load(n, src, dst):
        copy = pltpu.make_async_copy(src, dst, wsem.at[n])
        copy.start()
        return copy

    loads = {}
    for n, (name, src, dst) in enumerate(
        (
            ("pair", h_pair, pair), ("pgains", h_pgains, pgains), ("b", h_wb, wb),
            ("hom", h_hom, hom), ("scales", h_scales, scales),
        )
    ):
        loads[name] = load(14 + n, src, dst)

    loads["q"] = []
    for b in range(4):
        column = pl.multiple_of(256 * b + 128 * half, 128)
        loads["q"].append(load(b, h_wq.at[:, pl.ds(column, 128)], wq.at[:, pl.ds(128 * b, 128)]))
    for n, (name, src, dst) in enumerate(
        (
            ("f", h_wf, wf), ("v", h_wv, wv), ("vf", h_wvf, wvf), ("e", h_we, we), ("s", h_ws, ws),
            ("d", h_wd, wd), ("o", h_wo, wo), ("t", h_wt, wt), ("to", h_wto, wto),
        )
    ):
        loads[name] = [load(4 + n, src, dst)]

    def ready(name, src, dst):
        for copy in loads[name]:
            copy.wait()
        depth = src.shape[0]

        @pl.loop(0, depth // 32)
        def _(n):
            rows = pl.ds(pl.multiple_of(n * 32, 32), 32)
            hi, lo = split(src[rows, :])
            dst[0, rows, :] = hi
            dst[1, rows, :] = lo

    def weight(ref, rows=slice(None), columns=slice(None)):
        return ref[0, rows, columns], ref[1, rows, columns]

    def send(n, src, dst, device):
        pltpu.make_async_remote_copy(
            src_ref=src, dst_ref=dst, send_sem=ssem.at[n], recv_sem=rsem.at[n],
            device_id=device, device_id_type=MESH,
        ).start()

    def keep(n, src, dst):
        pltpu.make_async_copy(src, dst, rsem.at[n]).start()

    def exchange(n, me, device, src, dst):
        peers = gi_peers() if device is on_gi else bj_peers()
        each(peers, lambda peer: send(n, src(peer), dst, device(peer)))
        keep(n, src(me), dst)

    def far_first(one):
        @pl.loop(0, 7)
        def _(k):
            there = (z + jnp.where(k % 2 == 1, 4 - (k + 1) // 2, 4 + k // 2)) % 8
            one((1 - half) * 8 + there, False)
            one(half * 8 + there, False)

        one((1 - half) * 8 + z, False)
        one(gi, True)

    def eight(ref, b):
        return ref.at[:, pl.ds(pl.multiple_of(b * 8, 8), 8), :]

    def arrived(n, whole):
        pltpu.make_async_copy(whole, whole, rsem.at[n]).wait()

    def sent(n, most):
        pltpu.make_async_copy(most, most, ssem.at[n]).wait()

    for name in ("pair", "pgains", "b"):
        loads[name].wait()
    bias = f_bias(pair[...].reshape(256, 128), pgains[0:1, :], wb[...])
    s_bias1[0], s_bias1[1] = bias[:, :128], bias[:, 128:]
    pl.semaphore_wait(barrier, 30)
    exchange(1, gi, on_gi, lambda g: s_bias1.at[g // 8], r_bias1.at[gi])
    loads["hom"].wait()
    exchange(0, gi, on_gi, lambda g: hom.at[g % 8], r_raw.at[:, gi])
    ready("q", wq, bq)
    value = hom[...].reshape(128, 256)
    for n in range(2):
        lanes = slice(128 * n, 128 * n + 128)
        first[n] = value[:, lanes]
        for p in range(16):
            s_col[p, :, lanes] = first[n, pl.ds(p, 8, stride=16), :]
    arrived(1, r_bias1)
    turned = r_bias1[...].reshape(128, 128).T
    for ih in range(2):
        s_bias2[:, :, :, 128 * ih : 128 * ih + 128] = turned[64 * ih : 64 * ih + 64].reshape(4, 2, 8, 128)

    def slot(branch, j):
        return r_bias2.at[:, :, pl.ds(pl.multiple_of(branch * 64 + j * 8, 8), 8), :]

    def pass_on(n, src, j, device):
        pltpu.make_async_remote_copy(
            src_ref=src, dst_ref=slot(core, j), send_sem=ssem.at[2], recv_sem=bsem.at[n],
            device_id=device, device_id_type=MESH,
        ).start()

    sibling = {"branch": 1 - core}

    to = [(px * 2 + py) for px, py in gj_peers()]
    steps = sorted(((dx, dy) for dx in range(4) for dy in range(2)), key=lambda s: -s[1] - min(s[0], 4 - s[0]))
    senders = [((gx + 4 - dx) % 4 * 2 + flip(dy, gy)) for dx, dy in steps]
    for d in range(7):
        pass_on(d + 1, s_bias2, gj, {"gj": to[d]})
    pass_on(0, s_bias2, gj, sibling)
    keep(2, s_bias2, slot(core, gj))
    arrived(0, r_raw)
    loads["scales"].wait()
    x = norm(r_raw[...].reshape(256, 256), scales[0:1, :])
    p = mm(split(x), weight(bq))
    q, k, vt = split(p[:, :128]), split(p[:, 128:256]), split(p[:, 256:384].T)
    gate[...] = jax.nn.sigmoid(p[:, 384:])
    for h in range(4):
        scores[h] = head_scores(k, q, h)
    turned_v[0], turned_v[1] = vt

    for d in range(7):
        j = senders[d]
        pltpu.make_async_copy(slot(core, j), slot(core, j), bsem.at[d + 1]).wait()
        pass_on(8 + d, slot(core, j), j, sibling)

    exchange(4, bj, on_bj, lambda b: s_col.at[b], r_col.at[bj])
    ready("f", wf, bf)
    arrived(2, s_bias2)
    for n, j in enumerate([gj] + senders[:7]):
        pltpu.make_async_copy(slot(1 - core, j), slot(1 - core, j), bsem.at[7 + n if n else 0]).wait()
    vt = turned_v[0], turned_v[1]
    heads = [attend(scores[h] + r_bias2[h].reshape(256, 256), vt, h) for h in range(4)]
    att = gate[...] * jnp.concatenate(heads, axis=0).T
    s_att[:, 0, :] = att
    seat = r_att.at[half, pl.ds(bj * 8 + z, 1)]

    def to_columns(g, mine):
        for px, py in gj_peers():
            for c in (1, 0):
                there = flip(c, core)
                src = s_att.at[pl.ds(there * 128 + g * 8 + px * 2 + py, 1)]
                if mine and c == 0 and py is gy and (px is gx):
                    keep(3, src, seat)
                else:
                    send(3, src, seat, {"branch": there, "gi": g, "gj": px * 2 + py})

    far_first(to_columns)
    ready("v", wv, bv)
    ready("vf", wvf, bvf)
    ready("e", we, be)
    ready("s", ws, bs)

    arrived(3, r_att)
    col = mm(split(r_att[0, :, 0, :]), weight(bf, slice(0, 128)))
    col += mm(split(r_att[1, :, 0, :]), weight(bf, slice(128, 256)))
    first[0], first[1] = col[:, :128], col[:, 128:]
    arrived(4, r_col)
    col = r_col[...].reshape(128, 256) + jnp.concatenate([first[0], first[1]], axis=1)
    xs = split(norm(col, scales[1:2, :]))
    p = mm(xs, weight(bv))
    pieces = []
    for n in range(2):
        q, k, v, g = (p[:, 256 * b + 128 * n : 256 * b + 128 * n + 128] for b in range(4))
        q, k, vt, g = split(q), split(k), split(v.T), jax.nn.sigmoid(g)
        heads = [attend(head_scores(k, q, h), vt, h) for h in range(4)]
        pieces.append(g * jnp.concatenate(heads, axis=0).T)
    second = (
        col
        + mm(split(pieces[0]), weight(bvf, slice(0, 128)))
        + mm(split(pieces[1]), weight(bvf, slice(128, 256)))
    )
    wide = jax.nn.relu(mm(split(norm(second, scales[2:3, :])), weight(be)))
    al = second + mm(split(wide), weight(bs))
    s_al[0], s_al[1] = al[:, :128], al[:, 128:]
    for copy in loads["d"]:
        copy.wait()
    factors = mm(split(wd[...]), split(norm(al, scales[3:4, :])), NT)
    s_ab[...] = factors.reshape(2, 32, 128)

    each(gi_peers(), lambda g: send(6, s_ab.at[1], r_b.at[bj], cross(g)))

    @pl.when(gi == bj)
    def _():
        keep(6, s_ab.at[1], r_b.at[bj])

    @pl.when(gi != bj)
    def _():
        send(6, s_ab.at[1], r_b.at[bj], cross(gi))

    exchange(5, bj, on_bj, lambda b: s_ab.at[0], r_a.at[bj])

    exchange(7, bj, on_bj, lambda b: eight(s_al, b), eight(r_al, bj))
    ready("o", wo, bo)
    ready("t", wt, bt)
    ready("to", wto, bto)

    arrived(5, r_a)
    arrived(6, r_b)

    def outer_weight(g):
        parts = [weight(bo, slice(256 * g + 128 * n, 256 * g + 128 * n + 128)) for n in range(2)]
        return tuple(jnp.concatenate([parts[0][m], parts[1][m]], axis=1) for m in range(2))

    updates = f_opm(r_a[...].reshape(512, 128), r_b[...].reshape(512, 128), outer_weight)
    for n in range(2):
        rows = slice(8 * n, 8 * n + 8)
        pf[:, rows, :] = pair[:, rows, :] + updates[n]
    xs = split(norm(pf[...].reshape(256, 128), pgains[1:2, :]))
    p = mm(xs, weight(bt, columns=slice(0, 256)))
    factor = jax.nn.sigmoid(p[:, 128:]) * p[:, :128]
    for n in range(2):
        s_ta[n] = factor[128 * n : 128 * n + 128].T
    exchange(8, bj, on_bj, lambda b: eight(s_ta, b), eight(r_ta, bj))
    p = mm(xs, weight(bt, columns=slice(256, 512)))
    factor = jax.nn.sigmoid(p[:, 128:]) * p[:, :128]
    for n in range(2):
        s_tb[n] = factor[128 * n : 128 * n + 128].T
    exchange(9, bj, on_bj, lambda b: eight(s_tb, b), eight(r_tb, bj))
    gout[...] = jax.nn.sigmoid(mm(xs, weight(bt, columns=slice(512, 640))))

    def regroup(src, dst):
        for ih in range(2):
            for bh in range(2):
                block = jnp.stack([src[ih, pl.ds(64 * bh + c, 8, stride=8), :] for c in range(8)])
                dst[:, 8 * ih : 8 * ih + 8, 128 * bh : 128 * bh + 128] = swap_blocks(block, 3, 4)

    paired = core == half

    def to_channels(one):
        for dz in (4, 3, 5, 2, 6, 1, 7):
            one((z + dz) % 8)

        @pl.when(core != half)
        def _():
            one(z)

    def left(there):
        pltpu.make_async_remote_copy(
            src_ref=s_ba.at[there], dst_ref=r_ba.at[gi], send_sem=ssem.at[10], recv_sem=csem.at[gi],
            device_id={"gi": core * 8 + there}, device_id_type=MESH,
        ).start()

    def right(there):
        send(11, s_bb.at[there], r_bb.at[z], {"gi": core * 8 + there, "branch": half})

    arrived(8, r_ta)
    regroup(r_ta, s_ba)
    to_channels(left)

    @pl.when(paired)
    def _():
        pltpu.make_async_copy(s_ba.at[z], r_ba.at[gi], csem.at[gi]).start()

    arrived(9, r_tb)
    regroup(r_tb, s_bb)
    to_channels(right)

    @pl.when(paired)
    def _():
        keep(11, s_bb.at[z], r_bb.at[z])
        for dy in range(2):
            for dz in (0, 1, 7, 2, 6, 3, 5, 4):
                g = flip(dy, half) * 8 + (z + dz) % 8
                pltpu.make_async_copy(r_ba.at[g], r_ba.at[g], csem.at[g]).wait()
                pltpu.make_async_remote_copy(
                    src_ref=r_ba.at[g], dst_ref=r_ba.at[g], send_sem=ssem.at[10], recv_sem=rsem.at[10 + 4 * dy],
                    device_id=sibling, device_id_type=MESH,
                ).start()

    arrived(11, r_bb)
    place = r_d.at[:, pl.ds((half * 8 + gj) * 8 + z, 1)]

    def to_pairs(g, mine):
        for px, py in gj_peers():
            src = s_d.at[:, pl.ds(g * 8 + px * 2 + py, 1)]
            if mine and py is gy and px is gx:
                keep(13, src, place)
            else:
                send(13, src, place, {"gi": g, "gj": px * 2 + py})

    rights = split(r_bb[...].reshape(128, 256))
    for dy in range(2):
        there = flip(dy, half)
        rows = r_ba.at[pl.ds(there * 8, 8)]

        @pl.when(jnp.logical_not(paired))
        def _():
            arrived(10 + 4 * dy, rows)

        x = mm(split(rows[...].reshape(128, 256)), rights, NT).reshape(8, 2, 8, 128)
        for ih in range(2):
            s_d[ih, pl.ds(there * 64, 64), 0, :] = swap_blocks(x[:, ih], 3, 4).reshape(64, 128)

        @pl.loop(0, 7)
        def _(k):
            to_pairs(there * 8 + (z + jnp.where(k % 2 == 1, 4 - (k + 1) // 2, 4 + k // 2)) % 8, False)

        to_pairs(there * 8 + z, dy == 0)

    arrived(7, r_al)
    for row in range(8):
        for n in range(2):
            out_al[row, :, 128 * n : 128 * n + 128] = r_al[n, pl.ds(row, 16, stride=8), :]

    fifteen = pl.ds(0, 15)
    for n, ref in ((1, r_bias1), (4, s_col), (5, r_a)):
        sent(n, ref.at[fifteen])
    sent(0, r_raw.at[:, fifteen])
    sent(2, r_bias2.at[:, :, pl.ds(0, 120), :])
    for n, ref in ((7, s_al), (8, s_ta), (9, s_tb)):
        sent(n, ref.at[:, pl.ds(0, 120), :])
    sent(10, r_ba.at[pl.ds(0, 7)])

    @pl.when(paired)
    def _():
        sent(10, r_ba)

    @pl.when(jnp.logical_not(paired))
    def _():
        sent(10, r_ba.at[pl.ds(0, 1)])
        sent(11, r_bb.at[pl.ds(0, 1)])

    sent(11, r_bb.at[pl.ds(0, 7)])
    sent(6, r_b.at[fifteen])
    sent(3, s_att.at[pl.ds(0, 255)])

    @pl.when(gi != bj)
    def _():
        sent(6, r_b.at[pl.ds(0, 1)])

    arrived(13, r_d)
    x = norm(jnp.concatenate([r_d[0, :, 0, :].T, r_d[1, :, 0, :].T], axis=0), pgains[2:3, :])
    y = pf[...].reshape(256, 128) + gout[...] * mm(split(x), weight(bto))
    out_pair[...] = y.reshape(16, 16, 128)

    sent(13, s_d.at[:, pl.ds(0, 127)])


def solution(mesh):
    def vmem(*shape, dtype=F32):
        return pltpu.VMEM(shape, dtype)

    widths = (
        (256, 512), (256, 256), (256, 1024), (256, 256), (256, 1024), (1024, 256), (64, 256),
        (1024, 128), (128, 640), (128, 128),
    )
    small = ((8, 2, 8, 256), (16, 16, 128), (4, 256), (3, 128), (8, 128))
    scratch = [vmem(*w) for w in small + widths]
    scratch += [vmem(2, *w, dtype=BF16) for w in widths if w != (64, 256)] + [
        vmem(2, 8, 128), vmem(16, 8, 128), vmem(4, 2, 8, 256), vmem(4, 2, 128, 256), vmem(2, 16, 8, 256),
        vmem(256, 128), vmem(4, 256, 256), vmem(2, 128, 256, dtype=BF16),
        vmem(256, 1, 128), vmem(2, 128, 1, 128), vmem(2, 128, 128), vmem(16, 8, 256), vmem(16, 8, 256),
        vmem(2, 128, 128), vmem(2, 128, 128), vmem(2, 32, 128), vmem(16, 32, 128), vmem(16, 32, 128),
        vmem(16, 16, 128), vmem(256, 128), vmem(2, 128, 128), vmem(2, 128, 128), vmem(2, 128, 128), vmem(2, 128, 128),
        vmem(8, 16, 256), vmem(8, 16, 256), vmem(16, 16, 256), vmem(8, 16, 256),
        vmem(2, 128, 1, 128), vmem(2, 128, 1, 128),
        pltpu.SemaphoreType.DMA((19,)), pltpu.SemaphoreType.DMA((14,)), pltpu.SemaphoreType.DMA((15,)),
        pltpu.SemaphoreType.DMA((15,)), pltpu.SemaphoreType.DMA((16,)),
    ]

    def per_device(*args):
        args = list(args)
        args[0] = args[0].reshape(8, 2, 8, 256)
        args[4], args[11] = args[4].T, args[11].T
        return pl.pallas_call(
            kernel,
            out_shape=(
                pltpu.VMEM((8, 16, 256), F32),
                pltpu.VMEM((16, 16, 128), F32),
            ),
            in_specs=[pl.BlockSpec(memory_space=pl.ANY)] * 15,
            out_specs=(pl.BlockSpec(memory_space=pltpu.VMEM),) * 2,
            scratch_shapes=scratch,
            compiler_params=pltpu.CompilerParams(
                collective_id=0, has_side_effects=True, vmem_limit_bytes=56 * 1024 * 1024
            ),
            name="block",
        )(*args)

    msa, pairs = P(("branch", "gj"), "gi", None), P("gi", ("branch", "gj"), None)
    return jax.shard_map(
        per_device, mesh=mesh, in_specs=(msa, pairs) + (P(),) * 13, out_specs=(msa, pairs), check_vma=False
    )
```
